32 devices in a mesh: wide: 16 (over z, y, core), narrow: 2 (over x).
Axes of the slice: x: 2, y: 2, z: 4, core: 2. Of those that a mesh axis runs over, the one named last changes fastest.
Arguments:
- tokens: bfloat16 [32768, 768], P(('wide', 'narrow')), may hold values from -6 to 6
- init_memory: bfloat16 [64, 10, 768], P(('wide', 'narrow')), may hold values from -6 to 6
- w_query: bfloat16 [589824], P(('wide', 'narrow')), may hold values from -0.21875 to 0.21875
- w_key: bfloat16 [589824], P(('wide', 'narrow')), may hold values from -0.21875 to 0.21875
- w_value: bfloat16 [589824], P(('wide', 'narrow')), may hold values from -0.21875 to 0.21875
- w_output: bfloat16 [589824], P(('wide', 'narrow')), may hold values from -3 to 3
- w_inner: bfloat16 [2359296], P(('wide', 'narrow')), may hold values from -0.21875 to 0.21875
- w_outer: bfloat16 [2359296], P(('wide', 'narrow')), may hold values from -0.109375 to 0.109375
- vectors: bfloat16 [9216], P(('wide', 'narrow'))
- chain_start: int32 [64], P(('wide', 'narrow')), may hold values from 0 to 1, as said below
- true_count: int32 [64], P(('wide', 'narrow')), may hold values from 128 to 512, as said below
- cotangent: bfloat16 [32768, 768], P(('wide', 'narrow')), may hold values from -6 to 6
Outputs:
- mixed: bfloat16 [32768, 768], P(('wide', 'narrow'))
- grad_tokens: float32 [32768, 768], P(('wide', 'narrow'))
- grad_memory: float32 [64, 10, 768], P(('wide', 'narrow'))
- grad_query: float32 [589824], P(('wide', 'narrow'))
- grad_key: float32 [589824], P(('wide', 'narrow'))
- grad_value: float32 [589824], P(('wide', 'narrow'))
- grad_output: float32 [589824], P(('wide', 'narrow'))
- grad_inner: float32 [2359296], P(('wide', 'narrow'))
- grad_outer: float32 [2359296], P(('wide', 'narrow'))
- grad_vectors: float32 [9216], P(('wide', 'narrow'))
The draws below stay inside these ranges and needn't reach their ends.
Inputs may be any that keep to these rules, and one draw needn't show every extreme that they name: `chain_start`: the first segment of each aligned block of 2 segments begins a chain, so no chain crosses such a block; a later segment of a block may begin a new chain or continue the chain before; segment 1 continues segment 0. `true_count`: every segment that is followed by a continuation of its chain is full; the last segment of a chain may be partly padded, and segment 64 - 1 holds exactly 128 true tokens.
All inputs are finite; a program needn't handle non-finite values.
Results may differ from the reference program's by a relative error of at most 0.014.
Values may be sent and summed in bfloat16 or wider, within the bound.
No kernel may reach another device: no remote copies, remote signals or barrier semaphores. Data moves between devices by JAX's collectives and lax.ppermute only.
A program may use at most 256 MiB of HBM per device.

```python
import math
import jax
import jax.numpy as jnp
from jax import lax

D = 768
HEADS = 12
HEAD_DIM = 64
FF = 3072
SEG = 512
MEM = 10
SEG_DEV = 2
ROWS = 532
NSEG = 64
TOKENS = 32768


def chain_layout(key):
    indices = jnp.arange(NSEG)
    coin = jax.random.randint(jax.random.fold_in(key, 41), (NSEG,), 0, 2)
    starts = jnp.where(indices % SEG_DEV == 0, 1, coin)
    starts = jnp.where(indices == 1, 0, starts)
    return starts.astype(jnp.int32)


def draw_chain_start(key, part):
    return chain_layout(key)


def draw_true_count(key, part):
    starts = chain_layout(key)
    following = jnp.concatenate([starts[1:], jnp.ones((1,), jnp.int32)])
    count_key = jax.random.fold_in(key, 23)
    counts = jax.random.randint(count_key, (NSEG,), SEG // 4, SEG + 1)
    counts = jnp.where(following == 1, counts, SEG)
    indices = jnp.arange(NSEG)
    counts = jnp.where(indices == NSEG - 1, SEG // 4, counts)
    return counts.astype(jnp.int32)


def draw_vectors(key, part):
    total = 8 * D + FF
    noise = jax.random.normal(jax.random.fold_in(key, 3), (total,), jnp.float32)
    spread = jax.random.uniform(jax.random.fold_in(key, 5), (total,), jnp.float32, 0.6, 1.4)
    indices = jnp.arange(total)
    group = indices // D
    is_gain = ((group == 3) | (group == 6)) & (indices < 8 * D)
    values = jnp.where(is_gain, spread, 0.3 * jnp.clip(noise, -4.0, 4.0))
    return values.astype(jnp.bfloat16)


def shard_levels(rng, shape, shards, least, top_value):
    def one(dim, blocks):
        steps = jax.random.uniform(jax.random.fold_in(jax.random.fold_in(rng, 6), dim), (blocks,), jnp.float32, least / len(shards), top_value / len(shards))
        return jnp.repeat(jnp.exp(steps), shape[dim] // blocks).reshape((-1,) + (1,) * (len(shape) - dim - 1))

    level = one(*shards[0])
    for cut in shards[1:]:
        level = level * one(*cut)
    return level


def bell_draw(rng, dims, deviation, most, split=(), kind=jnp.bfloat16):
    factor_of = shard_levels(rng, dims, split, -0.22, 0.18) if split else 1.0
    drawn = jax.random.normal(rng, dims, jnp.float32) * deviation * factor_of
    return jnp.minimum(jnp.maximum(drawn, -most), most).astype(kind)


def setup_inputs(seed: int = 0) -> dict:
    splits = jax.random.split(jax.random.key(seed), 13)
    return {
        "tokens": bell_draw(splits[0], (TOKENS, D), 1.0, 6.0, ((0, 32),)),
        "init_memory": bell_draw(splits[1], (NSEG, MEM, D), 1.0, 6.0, ((0, 32),)),
        "w_query": bell_draw(splits[2], (D * D,), D ** -0.5, 0.21875, ((0, 32),)),
        "w_key": bell_draw(splits[3], (D * D,), D ** -0.5, 0.21875, ((0, 32),)),
        "w_value": bell_draw(splits[4], (D * D,), D ** -0.5, 0.21875, ((0, 32),)),
        "w_output": bell_draw(splits[5], (D * D,), (max(1, 3 * D // ROWS)) ** -0.5, 3.0, ((0, 32),)),
        "w_inner": bell_draw(splits[6], (D * FF,), D ** -0.5, 0.21875, ((0, 32),)),
        "w_outer": bell_draw(splits[7], (FF * D,), FF ** -0.5, 0.109375, ((0, 32),)),
        "vectors": draw_vectors(jax.random.fold_in(splits[12], 71), 0),
        "chain_start": draw_chain_start(jax.random.fold_in(splits[12], 71), 0),
        "true_count": draw_true_count(jax.random.fold_in(splits[12], 71), 0),
        "cotangent": bell_draw(splits[11], (TOKENS, D), 1.0, 6.0, ((0, 32),)),
    }


EPS = 1e-06
PRECISE = lax.Precision.HIGHEST

@jax.custom_vjp
def low(v):
    return lax.optimization_barrier(v.astype(jnp.bfloat16)).astype(jnp.float32)

@jax.custom_vjp
def low_back(v):
    return v

def low_keep(v):
    return (low(v), None)

def low_pass(kept, grad):
    return (grad,)

def back_keep(v):
    return (v, None)

def back_low(kept, grad):
    return (low(grad),)
low.defvjp(low_keep, low_pass)
low_back.defvjp(back_keep, back_low)

def layer_norm(hidden_in, gain, shift):
    average = lax.optimization_barrier(jnp.mean(hidden_in, axis=-1, keepdims=True))
    centred = hidden_in - average
    variance = lax.optimization_barrier(jnp.mean(centred * centred, axis=-1, keepdims=True))
    return centred * lax.rsqrt(variance + EPS) * gain + shift

def matmul(left, right):
    return jnp.dot(left, right, precision=PRECISE)

def segment(hidden_in, key_ok, matrices, vector_parts):
    w_query, w_key, w_value, w_output, w_inner, w_outer = matrices
    row_count = hidden_in.shape[0]
    scaling = 1.0 / math.sqrt(HEAD_DIM)
    low_hidden = low(hidden_in)
    queries = low_back(low(matmul(low_hidden, w_query) + vector_parts[0]))
    key_rows = low_back(low(matmul(low_hidden, w_key)))
    value_rows = low_back(low(matmul(low_hidden, w_value) + vector_parts[1]))
    head_queries = queries.reshape(row_count, HEADS, HEAD_DIM)
    head_keys = key_rows.reshape(row_count, HEADS, HEAD_DIM)
    head_values = value_rows.reshape(row_count, HEADS, HEAD_DIM)
    raw_scores = low_back(jnp.einsum('qhd,khd->hqk', head_queries, head_keys, precision=PRECISE))
    scores = jnp.where(key_ok[None, None, :], raw_scores * scaling, -1e+30)
    row_max = lax.optimization_barrier(jnp.max(scores, axis=-1, keepdims=True))
    exponent = jnp.exp(scores - row_max)
    probabilities = exponent / lax.optimization_barrier(jnp.sum(exponent, axis=-1, keepdims=True))
    attended = jnp.einsum('hqk,khd->qhd', low(probabilities), head_values, precision=PRECISE)
    attended = low_back(low(attended.reshape(row_count, D)))
    branch_one = low_back(matmul(attended, w_output) + vector_parts[2])
    hidden_one = layer_norm(hidden_in + branch_one, vector_parts[3], vector_parts[4])
    pre_act = low_back(matmul(low(hidden_one), w_inner) + vector_parts[8])
    activated = low(jax.nn.gelu(pre_act, approximate=False))
    branch_two = low_back(matmul(activated, w_outer) + vector_parts[5])
    return layer_norm(hidden_one + branch_two, vector_parts[6], vector_parts[7])

def reference(tokens, init_memory, w_query, w_key, w_value, w_output, w_inner, w_outer, vectors, chain_start, true_count, cotangent):
    positions = jnp.arange(SEG, dtype=jnp.int32)
    present = (positions[None, :] < true_count[:, None]).astype(jnp.float32)

    def forward(tok_rows, memory_in, query_w, key_w, value_w, output_w, inner_w, outer_w, vector_all):
        matrices = (query_w.reshape(D, D), key_w.reshape(D, D), value_w.reshape(D, D), output_w.reshape(D, D), inner_w.reshape(D, FF), outer_w.reshape(FF, D))
        vector_parts = [vector_all[index * D:(index + 1) * D] for index in range(8)] + [vector_all[8 * D:]]

        def step(carry, item):
            seg_tokens, seg_memory, starting, valid = item
            memory = jnp.where(starting > 0, seg_memory, carry)
            rows_in = jnp.concatenate([memory, seg_tokens * valid[:, None], memory], axis=0)
            key_ok = jnp.concatenate([jnp.ones((MEM,), jnp.bool_), valid > 0, jnp.ones((MEM,), jnp.bool_)])
            result = segment(rows_in, key_ok, matrices, vector_parts)
            return (result[MEM + SEG:], result[MEM:MEM + SEG] * valid[:, None])
        start_mem = jnp.zeros((MEM, D), jnp.float32)
        items = (tok_rows.reshape(NSEG, SEG, D), memory_in, chain_start, present)
        unused, token_out = lax.scan(jax.checkpoint(step), start_mem, items)
        return token_out.reshape(TOKENS, D)
    primals = tuple((arr.astype(jnp.float32) for arr in (tokens, init_memory, w_query, w_key, w_value, w_output, w_inner, w_outer, vectors)))
    token_out, pullback = jax.vjp(forward, *primals)
    grads = pullback(cotangent.astype(jnp.float32))
    return (token_out.astype(jnp.bfloat16), grads[0], grads[1], grads[2], grads[3], grads[4], grads[5], grads[6], grads[7], grads[8])
```

```python
import functools
import math

import jax
import jax.numpy as jnp
from jax import lax
from jax.experimental import pallas as pl
from jax.experimental.pallas import tpu as pltpu
from jax.sharding import PartitionSpec as P

D = 768
HEADS = 12
HEAD_DIM = 64
FF = 3072
SEG = 512
MEM = 10
EPS = 1e-06

MPAD = 16
R = SEG + MPAD
KEYS = 640
QUAD = 256
NQ = D // QUAD
BF = 512
NF = FF // BF
NEG = -1e30
EXP_SCALE = math.log2(math.e) / math.sqrt(HEAD_DIM)
F32 = jnp.float32
BF16 = jnp.bfloat16
VMEM_LIMIT = 60 * 1024 * 1024


def nt(a, b):
    return lax.dot_general(a, b, (((1,), (1,)), ((), ())), preferred_element_type=F32)


def tn(a, b):
    return lax.dot_general(a, b, (((0,), (0,)), ((), ())), preferred_element_type=F32)


def nn(a, b):
    return jnp.dot(a, b, preferred_element_type=F32)


def col_sum(v):
    return jnp.sum(v, axis=0, keepdims=True)


def row_mean(v):
    return jnp.mean(v, axis=-1, keepdims=True)


def row_ids(rows, cols):
    return lax.broadcasted_iota(jnp.int32, (rows, cols), 0)


def attn_fwd_kernel(
    count_ref, tok_ref, mem_ref, wq_ref, wk_ref, wv_ref, wo_ref, vq_ref, vec_ref,
    hb_ref, q_ref, k_ref, v_ref, o_ref, linv_ref, e_ref, xhat_ref, rstd_ref,
    h_s, k_s, v_s, acc_s,
):
    step = pl.program_id(0)
    count = count_ref[0]

    @pl.when(step == 0)
    def _():
        live = row_ids(SEG, D) < count
        h_s[0:SEG, :] = jnp.where(live, tok_ref[...].astype(F32), 0.0)
        h_s[SEG:R, :] = mem_ref[...]
        hb_ref[...] = h_s[...].astype(BF16)
        k_s[R:KEYS, :] = jnp.zeros((KEYS - R, QUAD), BF16)
        v_s[R:KEYS, :] = jnp.zeros((KEYS - R, QUAD), BF16)

    hb = hb_ref[...]
    q4 = (nn(hb, wq_ref[...]) + vq_ref[0:1, :]).astype(BF16)
    k4 = nn(hb, wk_ref[...]).astype(BF16)
    v4 = (nn(hb, wv_ref[...]) + vq_ref[1:2, :]).astype(BF16)
    q_ref[...] = q4
    k_ref[...] = k4
    v_ref[...] = v4
    k_s[0:R, :] = k4
    v_s[0:R, :] = v4
    key = lax.broadcasted_iota(jnp.int32, (1, KEYS), 1)
    bias = jnp.where(key < count, 0.0, NEG)
    twice = math.log(2.0) * math.sqrt(HEAD_DIM)
    bias = jnp.where((key >= SEG) & (key < SEG + MEM), twice, bias)
    first = lax.broadcasted_iota(jnp.int32, (1, 128), 1) < HEAD_DIM
    one = jnp.ones((KEYS, 128), BF16)
    for pair in range(2):
        lanes = slice(128 * pair, 128 * pair + 128)
        q2 = q4[:, lanes]
        k2 = k_s[:, lanes]
        vx = jnp.concatenate([v_s[:, lanes], one], axis=1)
        outs = []
        for half in range(2):
            mine = first if half == 0 else jnp.logical_not(first)
            qh = jnp.where(mine, q2, jnp.zeros_like(q2))
            s = nt(qh, k2) + bias
            top = jnp.max(s, axis=-1, keepdims=True)
            e = jnp.exp2((s - top) * EXP_SCALE).astype(BF16)
            e_ref[2 * pair + half] = e
            outs.append(nn(e, vx))
        num = jnp.where(first, outs[0][:, :128], outs[1][:, :128])
        den = jnp.where(first, outs[0][:, 128:], outs[1][:, 128:])
        inv = 1.0 / den
        linv_ref[:, lanes] = inv
        o_ref[:, lanes] = (num * inv).astype(BF16)
    part = nn(o_ref[...], wo_ref[...])

    @pl.when(step == 0)
    def _():
        acc_s[...] = part

    @pl.when(step > 0)
    def _():
        acc_s[...] = acc_s[...] + part

    @pl.when(step == NQ - 1)
    def _():
        r = h_s[...] + (acc_s[...] + vec_ref[2:3, :])
        c = r - row_mean(r)
        rstd = lax.rsqrt(row_mean(c * c) + EPS)
        xhat_ref[...] = c * rstd
        rstd_ref[...] = jnp.broadcast_to(rstd, (R, 128))


def const(shape):
    return pl.BlockSpec(shape, lambda j, *_: (0,) * len(shape))


def cols(rows, width):
    return pl.BlockSpec((rows, width), lambda j, *_: (0, j))


def rows(height, width):
    return pl.BlockSpec((height, width), lambda j, *_: (j, 0))


def sds(shape, dtype):
    return jax.ShapeDtypeStruct(shape, dtype)


def params():
    return pltpu.CompilerParams(
        dimension_semantics=("arbitrary",), vmem_limit_bytes=VMEM_LIMIT
    )


def attn_fwd(count, tok, mem, wq, wk, wv, wo, vecs):
    return pl.pallas_call(
        attn_fwd_kernel,
        grid_spec=pltpu.PrefetchScalarGridSpec(
            num_scalar_prefetch=1,
            grid=(NQ,),
            in_specs=[
                const((SEG, D)), const((MPAD, D)),
                cols(D, QUAD), cols(D, QUAD), cols(D, QUAD), rows(QUAD, D),
                cols(8, QUAD), const((8, D)),
            ],
            out_specs=[
                const((R, D)), cols(R, QUAD), cols(R, QUAD), cols(R, QUAD), cols(R, QUAD),
                cols(R, QUAD),
                pl.BlockSpec((4, R, KEYS), lambda j, *_: (j, 0, 0)),
                const((R, D)), const((R, 128)),
            ],
            scratch_shapes=[
                pltpu.VMEM((R, D), F32), pltpu.VMEM((KEYS, QUAD), BF16),
                pltpu.VMEM((KEYS, QUAD), BF16), pltpu.VMEM((R, D), F32),
            ],
        ),
        out_shape=[
            sds((R, D), BF16), sds((R, D), BF16), sds((R, D), BF16), sds((R, D), BF16),
            sds((R, D), BF16), sds((R, D), F32), sds((HEADS, R, KEYS), BF16),
            sds((R, D), F32), sds((R, 128), F32),
        ],
        compiler_params=params(),
        name="attn_fwd",
    )(count, tok, mem, wq, wk, wv, wo, vecs, vecs)


def ffn_fwd_kernel(
    count_ref, xhat_ref, wi_ref, bi_ref, wo_ref, vec_ref,
    h1b_ref, g_ref, gp_ref, mixed_ref, write_ref, xhat2_ref, rstd2_ref,
    acc_s,
):
    step = pl.program_id(0)

    @pl.when(step == 0)
    def _():
        h1b_ref[...] = (xhat_ref[...] * vec_ref[3:4, :] + vec_ref[4:5, :]).astype(BF16)

    f1 = nn(h1b_ref[...], wi_ref[...]) + bi_ref[...]
    cdf = 0.5 * (1.0 + lax.erf(f1 * math.sqrt(0.5)))
    pdf = jnp.exp(-0.5 * f1 * f1) * (1.0 / math.sqrt(2.0 * math.pi))
    g = (f1 * cdf).astype(BF16)
    g_ref[...] = g
    gp_ref[...] = (cdf + f1 * pdf).astype(BF16)
    part = nn(g, wo_ref[...])

    @pl.when(step == 0)
    def _():
        acc_s[...] = part

    @pl.when(step > 0)
    def _():
        acc_s[...] = acc_s[...] + part

    @pl.when(step == NF - 1)
    def _():
        h1 = xhat_ref[...] * vec_ref[3:4, :] + vec_ref[4:5, :]
        r = h1 + (acc_s[...] + vec_ref[5:6, :])
        c = r - row_mean(r)
        rstd = lax.rsqrt(row_mean(c * c) + EPS)
        xhat = c * rstd
        xhat2_ref[...] = xhat
        rstd2_ref[...] = jnp.broadcast_to(rstd, (R, 128))
        y = xhat * vec_ref[6:7, :] + vec_ref[7:8, :]
        live = row_ids(SEG, D) < count_ref[0]
        mixed_ref[...] = jnp.where(live, y[0:SEG, :], 0.0).astype(BF16)
        write_ref[...] = jnp.where(row_ids(MPAD, D) < MEM, y[SEG:R, :], 0.0)


def ffn_fwd(count, xhat, wi, bi, wo, vecs):
    return pl.pallas_call(
        ffn_fwd_kernel,
        grid_spec=pltpu.PrefetchScalarGridSpec(
            num_scalar_prefetch=1,
            grid=(NF,),
            in_specs=[const((R, D)), cols(D, BF), cols(1, BF), rows(BF, D), const((8, D))],
            out_specs=[
                const((R, D)), cols(R, BF), cols(R, BF), const((SEG, D)), const((MPAD, D)),
                const((R, D)), const((R, 128)),
            ],
            scratch_shapes=[pltpu.VMEM((R, D), F32)],
        ),
        out_shape=[
            sds((R, D), BF16), sds((R, FF), BF16), sds((R, FF), BF16), sds((SEG, D), BF16),
            sds((MPAD, D), F32), sds((R, D), F32), sds((R, 128), F32),
        ],
        compiler_params=params(),
        name="ffn_fwd",
    )(count, xhat, wi, bi, wo, vecs)


def norm_pull(grad, gain, xhat, rstd):
    gx = grad * gain
    return rstd * (gx - row_mean(gx) - xhat * row_mean(gx * xhat))


def ffn_bwd_kernel(
    count_ref, cot_ref, gw_ref, xhat2_ref, rstd2_ref, xhat_ref, rstd_ref, wi_ref, wo_ref,
    gp_ref, vec_ref,
    df2_ref, df1_ref, dr1_ref, dr1b_ref, dbi_ref, dvec_ref,
    acc_s,
):
    step = pl.program_id(0)

    @pl.when(step == 0)
    def _():
        live = row_ids(SEG, D) < count_ref[0]
        acc_s[0:SEG, :] = jnp.where(live, cot_ref[...].astype(F32), 0.0)
        acc_s[SEG:R, :] = gw_ref[...]
        dy = acc_s[...]
        xhat2 = xhat2_ref[...]
        dvec_ref[6:7, :] = col_sum(dy * xhat2)
        dvec_ref[7:8, :] = col_sum(dy)
        dr2 = norm_pull(dy, vec_ref[6:7, :], xhat2, rstd2_ref[:, 0:1])
        df2 = dr2.astype(BF16)
        df2_ref[...] = df2
        dvec_ref[5:6, :] = col_sum(df2.astype(F32))
        acc_s[...] = dr2

    df1 = (nt(df2_ref[...], wo_ref[...]) * gp_ref[...].astype(F32)).astype(BF16)
    df1_ref[...] = df1
    dbi_ref[...] = col_sum(df1.astype(F32))
    acc_s[...] = acc_s[...] + nt(df1, wi_ref[...])

    @pl.when(step == NF - 1)
    def _():
        dh1 = acc_s[...]
        xhat = xhat_ref[...]
        dvec_ref[3:4, :] = col_sum(dh1 * xhat)
        dvec_ref[4:5, :] = col_sum(dh1)
        dr1 = norm_pull(dh1, vec_ref[3:4, :], xhat, rstd_ref[:, 0:1])
        dr1_ref[...] = dr1
        dr1b = dr1.astype(BF16)
        dr1b_ref[...] = dr1b
        dvec_ref[2:3, :] = col_sum(dr1b.astype(F32))
        dvec_ref[0:2, :] = jnp.zeros((2, D), F32)


def ffn_bwd(count, cot, gw, xhat2, rstd2, xhat, rstd, wi, wo, gp, vecs):
    return pl.pallas_call(
        ffn_bwd_kernel,
        grid_spec=pltpu.PrefetchScalarGridSpec(
            num_scalar_prefetch=1,
            grid=(NF,),
            in_specs=[
                const((SEG, D)), const((MPAD, D)), const((R, D)), const((R, 128)),
                const((R, D)), const((R, 128)), cols(D, BF), rows(BF, D), cols(R, BF),
                const((8, D)),
            ],
            out_specs=[
                const((R, D)), cols(R, BF), const((R, D)), const((R, D)), cols(1, BF),
                const((8, D)),
            ],
            scratch_shapes=[pltpu.VMEM((R, D), F32)],
        ),
        out_shape=[
            sds((R, D), BF16), sds((R, FF), BF16), sds((R, D), F32), sds((R, D), BF16),
            sds((1, FF), F32), sds((8, D), F32),
        ],
        compiler_params=params(),
        name="ffn_bwd",
    )(count, cot, gw, xhat2, rstd2, xhat, rstd, wi, wo, gp, vecs)


def attn_bwd_kernel(
    count_ref, dr1_ref, dr1b_ref, wq_ref, wk_ref, wv_ref, wo_ref, q_ref, k_ref, v_ref, o_ref,
    linv_ref, e_ref,
    dq_ref, dk_ref, dv_ref, dqb_ref, dvb_ref, gtok_ref, gmem_ref,
    k_s, v_s, acc_s,
):
    step = pl.program_id(0)

    @pl.when(step == 0)
    def _():
        k_s[R:KEYS, :] = jnp.zeros((KEYS - R, QUAD), BF16)
        v_s[R:KEYS, :] = jnp.zeros((KEYS - R, QUAD), BF16)
        acc_s[...] = dr1_ref[...]

    k_s[0:R, :] = k_ref[...]
    v_s[0:R, :] = v_ref[...]
    grad_o = nt(dr1b_ref[...], wo_ref[...]).astype(BF16).astype(F32) * linv_ref[...]
    grad_ob = grad_o.astype(BF16)
    term = (-(grad_o * o_ref[...].astype(F32))).astype(BF16)
    first = lax.broadcasted_iota(jnp.int32, (1, 128), 1) < HEAD_DIM
    one = jnp.ones((KEYS, 128), BF16)
    scaling = 1.0 / math.sqrt(HEAD_DIM)
    for pair in range(2):
        lanes = slice(128 * pair, 128 * pair + 128)
        q2 = q_ref[:, lanes]
        k2 = k_s[:, lanes]
        do2 = grad_ob[:, lanes]
        tm2 = term[:, lanes]
        vx = jnp.concatenate([v_s[:, lanes], one], axis=1)
        dqs, dks, dvs = [], [], []
        for half in range(2):
            mine = first if half == 0 else jnp.logical_not(first)
            zero = jnp.zeros_like(do2)
            lhs = jnp.concatenate([jnp.where(mine, do2, zero), jnp.where(mine, tm2, zero)], axis=1)
            e = e_ref[2 * pair + half]
            ds = (nt(lhs, vx) * e.astype(F32)).astype(BF16)
            dqs.append(nn(ds, k2))
            dks.append(tn(ds, q2))
            dvs.append(tn(e, do2))
        dq_ref[:, lanes] = (jnp.where(first, dqs[0], dqs[1]) * scaling).astype(BF16)
        dk_ref[:, lanes] = (jnp.where(first, dks[0], dks[1])[0:R, :] * scaling).astype(BF16)
        dv_ref[:, lanes] = jnp.where(first, dvs[0], dvs[1])[0:R, :].astype(BF16)
    dq = dq_ref[...]
    dv = dv_ref[...]
    dqb_ref[...] = col_sum(dq.astype(F32))
    dvb_ref[...] = col_sum(dv.astype(F32))
    part = nt(dq, wq_ref[...]) + nt(dk_ref[...], wk_ref[...]) + nt(dv, wv_ref[...])
    acc_s[...] = acc_s[...] + part

    @pl.when(step == NQ - 1)
    def _():
        live = row_ids(SEG, D) < count_ref[0]
        gtok_ref[...] = jnp.where(live, acc_s[0:SEG, :], 0.0)
        gmem_ref[...] = jnp.where(row_ids(MPAD, D) < MEM, acc_s[SEG:R, :], 0.0)


def attn_bwd(count, dr1, dr1b, wq, wk, wv, wo, q, k, v, o, linv, e):
    return pl.pallas_call(
        attn_bwd_kernel,
        grid_spec=pltpu.PrefetchScalarGridSpec(
            num_scalar_prefetch=1,
            grid=(NQ,),
            in_specs=[
                const((R, D)), const((R, D)),
                cols(D, QUAD), cols(D, QUAD), cols(D, QUAD), rows(QUAD, D),
                cols(R, QUAD), cols(R, QUAD), cols(R, QUAD), cols(R, QUAD), cols(R, QUAD),
                pl.BlockSpec((4, R, KEYS), lambda j, *_: (j, 0, 0)),
            ],
            out_specs=[
                cols(R, QUAD), cols(R, QUAD), cols(R, QUAD), cols(1, QUAD), cols(1, QUAD),
                const((SEG, D)), const((MPAD, D)),
            ],
            scratch_shapes=[
                pltpu.VMEM((KEYS, QUAD), BF16), pltpu.VMEM((KEYS, QUAD), BF16),
                pltpu.VMEM((R, D), F32),
            ],
        ),
        out_shape=[
            sds((R, D), BF16), sds((R, D), BF16), sds((R, D), BF16), sds((1, D), F32),
            sds((1, D), F32), sds((SEG, D), F32), sds((MPAD, D), F32),
        ],
        compiler_params=params(),
        name="attn_bwd",
    )(count, dr1, dr1b, wq, wk, wv, wo, q, k, v, o, linv, e)


AXES = ("wide", "narrow")


def wgrad(left, grad):
    return tn(left, grad).astype(BF16)


def per_device(
    tokens, init_memory, w_query, w_key, w_value, w_output, w_inner, w_outer, vectors,
    chain_start, true_count, cotangent,
):
    slots = chain_start.shape[0]
    parts = D * D // w_query.shape[0]
    own = D // parts
    row = jnp.pad(vectors, (0, 8 * D - vectors.shape[0])).reshape(8, D)
    local_attn = jnp.concatenate(
        [w.reshape(own, D) for w in (w_query, w_key, w_value, w_output)] + [row], axis=0
    )
    attn_all = lax.all_gather(local_attn, AXES, axis=0, tiled=False)
    local_ffn = jnp.concatenate(
        [w_inner.reshape(own, FF)[:, D * i : D * i + D] for i in range(FF // D)]
        + [w_outer.reshape(4 * own, D)],
        axis=0,
    )
    ffn_all = lax.all_gather(local_ffn, AXES, axis=0, tiled=False)
    wq, wk, wv, wo = (
        attn_all[:, own * i : own * i + own].reshape(D, D) for i in range(4)
    )
    vec_all = attn_all[:, 4 * own].reshape(parts, D)[:, : vectors.shape[0]].reshape(-1)
    vec_all = vec_all.astype(F32)
    vecs = vec_all[: 8 * D].reshape(8, D)
    bi = vec_all[8 * D :].reshape(1, FF)
    wi = jnp.concatenate(
        [ffn_all[:, own * i : own * i + own].reshape(D, D) for i in range(FF // D)], axis=1
    )
    wu = ffn_all[:, 4 * own :].reshape(FF, D)

    tok = tokens.reshape(slots, SEG, D)
    cot = cotangent.reshape(slots, SEG, D)
    init = jnp.pad(init_memory.astype(F32), ((0, 0), (0, MPAD - MEM), (0, 0)))
    carry = jnp.zeros((MPAD, D), F32)
    saved, mixed = [], []
    for s in range(slots):
        count = true_count[s : s + 1]
        memory = jnp.where(chain_start[s] > 0, init[s], carry)
        a = attn_fwd(count, tok[s], memory, wq, wk, wv, wo, vecs)
        f = ffn_fwd(count, a[7], wi, bi, wu, vecs)
        carry = f[4]
        mixed.append(f[3])
        saved.append((a, f))
    back = jnp.zeros((MPAD, D), F32)
    done = [None] * slots
    for s in reversed(range(slots)):
        count = true_count[s : s + 1]
        hb, q, k, v, o, linv, e, xhat, rstd = saved[s][0]
        h1b, g, gp, _, _, xhat2, rstd2 = saved[s][1]
        df2, df1, dr1, dr1b, dbi, dvec = ffn_bwd(
            count, cot[s], back, xhat2, rstd2, xhat, rstd, wi, wu, gp, vecs
        )
        dq, dk, dv, dqb, dvb, gtok, gmem = attn_bwd(
            count, dr1, dr1b, wq, wk, wv, wo, q, k, v, o, linv, e
        )
        starts = chain_start[s] > 0
        ginit = jnp.where(starts, gmem, 0.0)[:MEM]
        back = jnp.where(starts, 0.0, gmem)
        vec = jnp.concatenate([dqb, dvb, dvec[2:8]], axis=0).reshape(-1)
        vec = jnp.concatenate([vec, dbi.reshape(-1)])
        done[s] = (hb, o, h1b, g, df2, df1, dr1b, dq, dk, dv, gtok, ginit, vec)

    def both(i):
        return jnp.concatenate([d[i] for d in done], axis=0)

    hb, o, h1b, g, df2, df1, dr1b, dq, dk, dv = (both(i) for i in range(10))
    vec = sum(d[12] for d in done)
    g_inner = wgrad(h1b, df1).reshape(parts, own, FF)
    g_outer = wgrad(g, df2).reshape(parts, 4 * own, D)
    flat_ffn = jnp.concatenate(
        [g_inner[:, :, D * i : D * i + D] for i in range(FF // D)] + [g_outer], axis=1
    )
    ffn_mine = lax.psum_scatter(flat_ffn, AXES, scatter_dimension=0, tiled=False)
    squares = [wgrad(hb, dq), wgrad(hb, dk), wgrad(hb, dv), wgrad(o, dr1b)]
    flat_attn = jnp.concatenate([w.reshape(parts, own, D) for w in squares], axis=1)
    attn_mine = lax.psum_scatter(flat_attn, AXES, scatter_dimension=0, tiled=False)
    vec_mine = lax.psum_scatter(vec, AXES, scatter_dimension=0, tiled=True)
    inner_mine = jnp.concatenate(
        [ffn_mine[own * i : own * i + own] for i in range(FF // D)], axis=1
    )
    return (
        jnp.concatenate(mixed, axis=0),
        both(10),
        jnp.stack([d[11] for d in done]),
        *(attn_mine[own * i : own * i + own].reshape(-1).astype(F32) for i in range(4)),
        inner_mine.reshape(-1).astype(F32),
        ffn_mine[4 * own :].reshape(-1).astype(F32),
        vec_mine,
    )


def solution(mesh):
    flat = P(AXES)
    return jax.shard_map(
        per_device,
        mesh=mesh,
        in_specs=(P(AXES, None), P(AXES, None, None)) + (flat,) * 9 + (P(AXES, None),),
        out_specs=(P(AXES, None), P(AXES, None), P(AXES, None, None)) + (flat,) * 7,
        check_vma=False,
    )
```

```python
import functools
import math

import jax
import jax.numpy as jnp
from jax import lax
from jax.experimental import pallas as pl
from jax.experimental.pallas import tpu as pltpu
from jax.sharding import PartitionSpec as P

D = 768
HEADS = 12
HEAD_DIM = 64
FF = 3072
SEG = 512
MEM = 10
EPS = 1e-06

MPAD = 16
R = SEG + MPAD
KEYS = 640
QUAD = 256
NQ = D // QUAD
BF = 512
NF = FF // BF
NEG = -1e30
EXP_SCALE = math.log2(math.e) / math.sqrt(HEAD_DIM)
F32 = jnp.float32
BF16 = jnp.bfloat16
VMEM_LIMIT = 60 * 1024 * 1024


def nt(a, b):
    return lax.dot_general(a, b, (((1,), (1,)), ((), ())), preferred_element_type=F32)


def tn(a, b):
    return lax.dot_general(a, b, (((0,), (0,)), ((), ())), preferred_element_type=F32)


def nn(a, b):
    return jnp.dot(a, b, preferred_element_type=F32)


def col_sum(v):
    return jnp.sum(v, axis=0, keepdims=True)


def row_mean(v):
    return jnp.mean(v, axis=-1, keepdims=True)


def row_ids(rows, cols):
    return lax.broadcasted_iota(jnp.int32, (rows, cols), 0)


def attn_fwd_kernel(
    count_ref, tok_ref, mem_ref, wq_ref, wk_ref, wv_ref, wo_ref, vq_ref, vec_ref,
    hb_ref, q_ref, k_ref, v_ref, o_ref, linv_ref, e_ref, xhat_ref, rstd_ref,
    h_s, k_s, v_s, acc_s,
):
    step = pl.program_id(0)
    count = count_ref[0]

    @pl.when(step == 0)
    def _():
        live = row_ids(SEG, D) < count
        h_s[0:SEG, :] = jnp.where(live, tok_ref[...].astype(F32), 0.0)
        h_s[SEG:R, :] = mem_ref[...]
        hb_ref[...] = h_s[...].astype(BF16)
        k_s[R:KEYS, :] = jnp.zeros((KEYS - R, QUAD), BF16)
        v_s[R:KEYS, :] = jnp.zeros((KEYS - R, QUAD), BF16)

    hb = hb_ref[...]
    q4 = (nn(hb, wq_ref[...]) + vq_ref[0:1, :]).astype(BF16)
    k4 = nn(hb, wk_ref[...]).astype(BF16)
    v4 = (nn(hb, wv_ref[...]) + vq_ref[1:2, :]).astype(BF16)
    q_ref[...] = q4
    k_ref[...] = k4
    v_ref[...] = v4
    k_s[0:R, :] = k4
    v_s[0:R, :] = v4
    key = lax.broadcasted_iota(jnp.int32, (1, KEYS), 1)
    bias = jnp.where(key < count, 0.0, NEG)
    twice = math.log(2.0) * math.sqrt(HEAD_DIM)
    bias = jnp.where((key >= SEG) & (key < SEG + MEM), twice, bias)
    first = lax.broadcasted_iota(jnp.int32, (1, 128), 1) < HEAD_DIM
    one = jnp.ones((KEYS, 128), BF16)
    for pair in range(2):
        lanes = slice(128 * pair, 128 * pair + 128)
        q2 = q4[:, lanes]
        k2 = k_s[:, lanes]
        vx = jnp.concatenate([v_s[:, lanes], one], axis=1)
        outs = []
        for half in range(2):
            mine = first if half == 0 else jnp.logical_not(first)
            qh = jnp.where(mine, q2, jnp.zeros_like(q2))
            s = nt(qh, k2) + bias
            top = jnp.max(s, axis=-1, keepdims=True)
            e = jnp.exp2((s - top) * EXP_SCALE).astype(BF16)
            e_ref[2 * pair + half] = e
            outs.append(nn(e, vx))
        num = jnp.where(first, outs[0][:, :128], outs[1][:, :128])
        den = jnp.where(first, outs[0][:, 128:], outs[1][:, 128:])
        inv = 1.0 / den
        linv_ref[:, lanes] = inv
        o_ref[:, lanes] = (num * inv).astype(BF16)
    part = nn(o_ref[...], wo_ref[...])

    @pl.when(step == 0)
    def _():
        acc_s[...] = part

    @pl.when(step > 0)
    def _():
        acc_s[...] = acc_s[...] + part

    @pl.when(step == NQ - 1)
    def _():
        r = h_s[...] + (acc_s[...] + vec_ref[2:3, :])
        c = r - row_mean(r)
        rstd = lax.rsqrt(row_mean(c * c) + EPS)
        xhat_ref[...] = c * rstd
        rstd_ref[...] = jnp.broadcast_to(rstd, (R, 128))


def const(shape):
    return pl.BlockSpec(shape, lambda j, *_: (0,) * len(shape))


def cols(rows, width):
    return pl.BlockSpec((rows, width), lambda j, *_: (0, j))


def rows(height, width):
    return pl.BlockSpec((height, width), lambda j, *_: (j, 0))


def slot_const(slot):
    return pl.BlockSpec((R, D), lambda j, *_: (slot, 0))


def slot_cols(slot, width):
    return pl.BlockSpec((R, width), lambda j, *_: (slot, j))


def any_spec():
    return pl.BlockSpec(memory_space=pl.ANY)


def sds(shape, dtype):
    return jax.ShapeDtypeStruct(shape, dtype)


def kept(n, kernel):
    def body(*refs):
        return kernel(*refs[:1], *refs[1 + n :])

    return body


def cost(flops, moved):
    return pl.CostEstimate(flops=flops, bytes_accessed=moved, transcendentals=0)


def params():
    return pltpu.CompilerParams(
        dimension_semantics=("arbitrary",), vmem_limit_bytes=VMEM_LIMIT
    )


def attn_fwd(slot, slots, prev, count, tok, mem, wqk, wvo, vecs):
    n = len(prev)
    return pl.pallas_call(
        kept(n, attn_fwd_kernel),
        grid_spec=pltpu.PrefetchScalarGridSpec(
            num_scalar_prefetch=1,
            grid=(NQ,),
            in_specs=[any_spec()] * n + [
                pl.BlockSpec((SEG, D), lambda j, *_: (slot, 0)), const((MPAD, D)),
                cols(D, QUAD), pl.BlockSpec((D, QUAD), lambda j, *_: (0, NQ + j)),
                cols(D, QUAD), pl.BlockSpec((QUAD, D), lambda j, *_: (j, 1)),
                cols(8, QUAD), const((8, D)),
            ],
            out_specs=[
                slot_const(slot), cols(R, QUAD), cols(R, QUAD), cols(R, QUAD),
                slot_cols(slot, QUAD),
                cols(R, QUAD),
                pl.BlockSpec((4, R, KEYS), lambda j, *_: (j, 0, 0)),
                const((R, D)), const((R, 128)),
            ],
            scratch_shapes=[
                pltpu.VMEM((R, D), F32), pltpu.VMEM((KEYS, QUAD), BF16),
                pltpu.VMEM((KEYS, QUAD), BF16), pltpu.VMEM((R, D), F32),
            ],
        ),
        out_shape=[
            sds((slots * R, D), BF16), sds((R, D), BF16), sds((R, D), BF16), sds((R, D), BF16),
            sds((slots * R, D), BF16), sds((R, D), F32), sds((HEADS, R, KEYS), BF16),
            sds((R, D), F32), sds((R, 128), F32),
        ],
        input_output_aliases={1: 0, 2: 4} if n else {},
        compiler_params=params(),
        cost_estimate=cost(2 * R * (4 * D * D + 2 * KEYS * D * 4), 20_000_000),
        name="attn_fwd",
    )(count, *prev, tok, mem, wqk, wqk, wvo, wvo, vecs, vecs)


def ffn_fwd_kernel(
    count_ref, xhat_ref, wi_ref, bi_ref, wo_ref, vec_ref,
    h1b_ref, g_ref, gp_ref, mixed_ref, write_ref, xhat2_ref, rstd2_ref,
    acc_s,
):
    step = pl.program_id(0)

    @pl.when(step == 0)
    def _():
        h1b_ref[...] = (xhat_ref[...] * vec_ref[3:4, :] + vec_ref[4:5, :]).astype(BF16)

    f1 = nn(h1b_ref[...], wi_ref[...]) + bi_ref[...]
    cdf = 0.5 * (1.0 + lax.erf(f1 * math.sqrt(0.5)))
    pdf = jnp.exp(-0.5 * f1 * f1) * (1.0 / math.sqrt(2.0 * math.pi))
    g = (f1 * cdf).astype(BF16)
    g_ref[...] = g
    gp_ref[...] = (cdf + f1 * pdf).astype(BF16)
    part = nn(g, wo_ref[...])

    @pl.when(step == 0)
    def _():
        acc_s[...] = part

    @pl.when(step > 0)
    def _():
        acc_s[...] = acc_s[...] + part

    @pl.when(step == NF - 1)
    def _():
        h1 = xhat_ref[...] * vec_ref[3:4, :] + vec_ref[4:5, :]
        r = h1 + (acc_s[...] + vec_ref[5:6, :])
        c = r - row_mean(r)
        rstd = lax.rsqrt(row_mean(c * c) + EPS)
        xhat = c * rstd
        xhat2_ref[...] = xhat
        rstd2_ref[...] = jnp.broadcast_to(rstd, (R, 128))
        y = xhat * vec_ref[6:7, :] + vec_ref[7:8, :]
        live = row_ids(SEG, D) < count_ref[0]
        mixed_ref[...] = jnp.where(live, y[0:SEG, :], 0.0).astype(BF16)
        write_ref[...] = jnp.where(row_ids(MPAD, D) < MEM, y[SEG:R, :], 0.0)


def ffn_fwd(slot, slots, prev, count, xhat, wi, bi, wo, vecs):
    n = len(prev)
    return pl.pallas_call(
        kept(n, ffn_fwd_kernel),
        grid_spec=pltpu.PrefetchScalarGridSpec(
            num_scalar_prefetch=1,
            grid=(NF,),
            in_specs=[any_spec()] * n + [const((R, D)), cols(D, BF), cols(1, BF), rows(BF, D), const((8, D))],
            out_specs=[
                slot_const(slot), slot_cols(slot, BF), cols(R, BF),
                pl.BlockSpec((SEG, D), lambda j, *_: (slot, 0)), const((MPAD, D)),
                const((R, D)), const((R, 128)),
            ],
            scratch_shapes=[pltpu.VMEM((R, D), F32)],
        ),
        out_shape=[
            sds((slots * R, D), BF16), sds((slots * R, FF), BF16), sds((R, FF), BF16),
            sds((slots * SEG, D), BF16),
            sds((MPAD, D), F32), sds((R, D), F32), sds((R, 128), F32),
        ],
        input_output_aliases={1: 0, 2: 1, 3: 3} if n else {},
        compiler_params=params(),
        cost_estimate=cost(2 * R * 2 * D * FF * 2, 20_000_000),
        name="ffn_fwd",
    )(count, *prev, xhat, wi, bi, wo, vecs)


def norm_pull(grad, gain, xhat, rstd):
    gx = grad * gain
    return rstd * (gx - row_mean(gx) - xhat * row_mean(gx * xhat))


def ffn_bwd_kernel(
    count_ref, cot_ref, gw_ref, xhat2_ref, rstd2_ref, xhat_ref, rstd_ref, wi_ref, wo_ref,
    gp_ref, vec_ref,
    df2_ref, df1_ref, dr1_ref, dr1b_ref, dbi_ref, dvec_ref,
    acc_s,
):
    step = pl.program_id(0)

    @pl.when(step == 0)
    def _():
        live = row_ids(SEG, D) < count_ref[0]
        acc_s[0:SEG, :] = jnp.where(live, cot_ref[...].astype(F32), 0.0)
        acc_s[SEG:R, :] = gw_ref[...]
        dy = acc_s[...]
        xhat2 = xhat2_ref[...]
        dvec_ref[6:7, :] = col_sum(dy * xhat2)
        dvec_ref[7:8, :] = col_sum(dy)
        dr2 = norm_pull(dy, vec_ref[6:7, :], xhat2, rstd2_ref[:, 0:1])
        df2 = dr2.astype(BF16)
        df2_ref[...] = df2
        dvec_ref[5:6, :] = col_sum(df2.astype(F32))
        acc_s[...] = dr2

    df1 = (nt(df2_ref[...], wo_ref[...]) * gp_ref[...].astype(F32)).astype(BF16)
    df1_ref[...] = df1
    dbi_ref[...] = col_sum(df1.astype(F32))
    acc_s[...] = acc_s[...] + nt(df1, wi_ref[...])

    @pl.when(step == NF - 1)
    def _():
        dh1 = acc_s[...]
        xhat = xhat_ref[...]
        dvec_ref[3:4, :] = col_sum(dh1 * xhat)
        dvec_ref[4:5, :] = col_sum(dh1)
        dr1 = norm_pull(dh1, vec_ref[3:4, :], xhat, rstd_ref[:, 0:1])
        dr1_ref[...] = dr1
        dr1b = dr1.astype(BF16)
        dr1b_ref[...] = dr1b
        dvec_ref[2:3, :] = col_sum(dr1b.astype(F32))
        dvec_ref[0:2, :] = jnp.zeros((2, D), F32)


def ffn_bwd(slot, slots, prev, count, cot, gw, xhat2, rstd2, xhat, rstd, wi, wo, gp, vecs):
    n = len(prev)
    return pl.pallas_call(
        kept(n, ffn_bwd_kernel),
        grid_spec=pltpu.PrefetchScalarGridSpec(
            num_scalar_prefetch=1,
            grid=(NF,),
            in_specs=[any_spec()] * n + [
                pl.BlockSpec((SEG, D), lambda j, *_: (slot, 0)), const((MPAD, D)), const((R, D)), const((R, 128)),
                const((R, D)), const((R, 128)), cols(D, BF), rows(BF, D), cols(R, BF),
                const((8, D)),
            ],
            out_specs=[
                slot_const(slot), slot_cols(slot, BF), const((R, D)), slot_const(slot),
                cols(1, BF), const((8, D)),
            ],
            scratch_shapes=[pltpu.VMEM((R, D), F32)],
        ),
        out_shape=[
            sds((slots * R, D), BF16), sds((slots * R, FF), BF16), sds((R, D), F32),
            sds((slots * R, D), BF16), sds((1, FF), F32), sds((8, D), F32),
        ],
        input_output_aliases={1: 0, 2: 1, 3: 3} if n else {},
        compiler_params=params(),
        cost_estimate=cost(2 * R * 2 * D * FF * 2, 20_000_000),
        name="ffn_bwd",
    )(count, *prev, cot, gw, xhat2, rstd2, xhat, rstd, wi, wo, gp, vecs)


def attn_bwd_kernel(
    count_ref, dr1_ref, dr1b_ref, wq_ref, wk_ref, wv_ref, wo_ref, q_ref, k_ref, v_ref, o_ref,
    linv_ref, e_ref,
    dq_ref, dk_ref, dv_ref, dqb_ref, dvb_ref, gtok_ref, gmem_ref,
    k_s, v_s, acc_s,
):
    step = pl.program_id(0)

    @pl.when(step == 0)
    def _():
        k_s[R:KEYS, :] = jnp.zeros((KEYS - R, QUAD), BF16)
        v_s[R:KEYS, :] = jnp.zeros((KEYS - R, QUAD), BF16)
        acc_s[...] = dr1_ref[...]

    k_s[0:R, :] = k_ref[...]
    v_s[0:R, :] = v_ref[...]
    grad_o = nt(dr1b_ref[...], wo_ref[...]).astype(BF16).astype(F32) * linv_ref[...]
    grad_ob = grad_o.astype(BF16)
    term = (-(grad_o * o_ref[...].astype(F32))).astype(BF16)
    first = lax.broadcasted_iota(jnp.int32, (1, 128), 1) < HEAD_DIM
    one = jnp.ones((KEYS, 128), BF16)
    scaling = 1.0 / math.sqrt(HEAD_DIM)
    for pair in range(2):
        lanes = slice(128 * pair, 128 * pair + 128)
        q2 = q_ref[:, lanes]
        k2 = k_s[:, lanes]
        do2 = grad_ob[:, lanes]
        tm2 = term[:, lanes]
        vx = jnp.concatenate([v_s[:, lanes], one], axis=1)
        dqs, dks, dvs = [], [], []
        for half in range(2):
            mine = first if half == 0 else jnp.logical_not(first)
            zero = jnp.zeros_like(do2)
            lhs = jnp.concatenate([jnp.where(mine, do2, zero), jnp.where(mine, tm2, zero)], axis=1)
            e = e_ref[2 * pair + half]
            ds = (nt(lhs, vx) * e.astype(F32)).astype(BF16)
            dqs.append(nn(ds, k2))
            dks.append(tn(ds, q2))
            dvs.append(tn(e, do2))
        dq_ref[:, lanes] = (jnp.where(first, dqs[0], dqs[1]) * scaling).astype(BF16)
        dk_ref[:, lanes] = (jnp.where(first, dks[0], dks[1])[0:R, :] * scaling).astype(BF16)
        dv_ref[:, lanes] = jnp.where(first, dvs[0], dvs[1])[0:R, :].astype(BF16)
    dq = dq_ref[...]
    dv = dv_ref[...]
    dqb_ref[...] = col_sum(dq.astype(F32))
    dvb_ref[...] = col_sum(dv.astype(F32))
    part = nt(dq, wq_ref[...]) + nt(dk_ref[...], wk_ref[...]) + nt(dv, wv_ref[...])
    acc_s[...] = acc_s[...] + part

    @pl.when(step == NQ - 1)
    def _():
        live = row_ids(SEG, D) < count_ref[0]
        gtok_ref[...] = jnp.where(live, acc_s[0:SEG, :], 0.0)
        gmem_ref[...] = jnp.where(row_ids(MPAD, D) < MEM, acc_s[SEG:R, :], 0.0)


def attn_bwd(slot, slots, prev, count, dr1, dr1b, wqk, wvo, q, k, v, o, linv, e):
    n = len(prev)
    return pl.pallas_call(
        kept(n, attn_bwd_kernel),
        grid_spec=pltpu.PrefetchScalarGridSpec(
            num_scalar_prefetch=1,
            grid=(NQ,),
            in_specs=[any_spec()] * n + [
                const((R, D)), slot_const(slot),
                cols(D, QUAD), pl.BlockSpec((D, QUAD), lambda j, *_: (0, NQ + j)),
                cols(D, QUAD), pl.BlockSpec((QUAD, D), lambda j, *_: (j, 1)),
                cols(R, QUAD), cols(R, QUAD), cols(R, QUAD), slot_cols(slot, QUAD),
                cols(R, QUAD),
                pl.BlockSpec((4, R, KEYS), lambda j, *_: (j, 0, 0)),
            ],
            out_specs=[
                slot_cols(slot, QUAD), slot_cols(slot, QUAD), slot_cols(slot, QUAD),
                cols(1, QUAD), cols(1, QUAD),
                pl.BlockSpec((SEG, D), lambda j, *_: (slot, 0)), const((MPAD, D)),
            ],
            scratch_shapes=[
                pltpu.VMEM((KEYS, QUAD), BF16), pltpu.VMEM((KEYS, QUAD), BF16),
                pltpu.VMEM((R, D), F32),
            ],
        ),
        out_shape=[
            sds((slots * R, D), BF16), sds((slots * R, D), BF16), sds((slots * R, D), BF16),
            sds((1, D), F32), sds((1, D), F32), sds((slots * SEG, D), F32), sds((MPAD, D), F32),
        ],
        input_output_aliases={1: 0, 2: 1, 3: 2, 4: 5} if n else {},
        compiler_params=params(),
        cost_estimate=cost(2 * R * (4 * D * D + 5 * KEYS * D * 4), 20_000_000),
        name="attn_bwd",
    )(count, *prev, dr1, dr1b, wqk, wqk, wvo, wvo, q, k, v, o, linv, e)


def wgrad_inner_kernel(core_ref, h_ref, da_ref, db_ref, mine_ref, theirs_ref):
    mine_ref[...] = tn(h_ref[...], da_ref[...]).astype(BF16)
    theirs_ref[...] = tn(h_ref[...], db_ref[...]).astype(BF16)


def wgrad_inner(core, h, d):
    depth, n = h.shape[0], FF // D // 2
    return pl.pallas_call(
        wgrad_inner_kernel,
        grid_spec=pltpu.PrefetchScalarGridSpec(
            num_scalar_prefetch=1,
            grid=(n,),
            in_specs=[
                const((depth, D)),
                pl.BlockSpec((depth, D), lambda j, c: (0, c[0] * n + j)),
                pl.BlockSpec((depth, D), lambda j, c: (0, (1 - c[0]) * n + j)),
            ],
            out_specs=[cols(D, D), cols(D, D)],
        ),
        out_shape=[sds((D, FF // 2), BF16)] * 2,
        compiler_params=params(),
        cost_estimate=cost(2 * depth * D * FF * 2, 15_000_000),
        name="wgrad_inner",
    )(core, h, d, d)


def wgrad_outer_kernel(core_ref, g_ref, d_ref, mine_ref, theirs_ref):
    full = tn(g_ref[...], d_ref[...]).astype(BF16)
    low = core_ref[0] == 0
    left, right = full[:, : D // 2], full[:, D // 2 :]
    mine_ref[...] = jnp.where(low, left, right)
    theirs_ref[...] = jnp.where(low, right, left)


def wgrad_outer(core, g, d):
    depth, n = g.shape[0], FF // D
    return pl.pallas_call(
        wgrad_outer_kernel,
        grid_spec=pltpu.PrefetchScalarGridSpec(
            num_scalar_prefetch=1,
            grid=(n,),
            in_specs=[cols(depth, D), const((depth, D))],
            out_specs=[rows(D, D // 2), rows(D, D // 2)],
        ),
        out_shape=[sds((FF, D // 2), BF16)] * 2,
        compiler_params=params(),
        cost_estimate=cost(2 * depth * D * FF * 2, 15_000_000),
        name="wgrad_outer",
    )(core, g, d)


def wgrad_attn_kernel(
    core_ref, hb_ref, o_ref, dq_ref, dk_ref, dv_ref, da_ref, qv_ref, vq_ref, ko_ref, ok_ref
):
    low = core_ref[0] == 0

    def put(mine_ref, theirs_ref, left, right):
        mine_ref[...] = jnp.where(low, left, right)
        theirs_ref[...] = jnp.where(low, right, left)

    dq, dk = tn(hb_ref[...], dq_ref[...]), tn(hb_ref[...], dk_ref[...])
    dv, do = tn(hb_ref[...], dv_ref[...]), tn(o_ref[...], da_ref[...])
    put(qv_ref, vq_ref, dq.astype(BF16), dv.astype(BF16))
    put(ko_ref, ok_ref, dk.astype(BF16), do.astype(BF16))


def wgrad_attn(core, hb, o, dq, dk, dv, da):
    depth, n = hb.shape[0], D // QUAD
    return pl.pallas_call(
        wgrad_attn_kernel,
        grid_spec=pltpu.PrefetchScalarGridSpec(
            num_scalar_prefetch=1,
            grid=(n,),
            in_specs=[const((depth, D))] * 2 + [cols(depth, QUAD)] * 4,
            out_specs=[cols(D, QUAD)] * 4,
        ),
        out_shape=[sds((D, D), BF16)] * 4,
        compiler_params=params(),
        cost_estimate=cost(2 * depth * D * D * 4 * 2, 15_000_000),
        name="wgrad_attn",
    )(core, hb, o, dq, dk, dv, da)


def strides(size):
    return [1 << i for i in reversed(range(size.bit_length() - 1))]


def after(value, *others):
    return lax.optimization_barrier((value, others))[0]


class Cube:
    def __init__(self, wide, narrow):
        self.size = {"wide": wide, "narrow": narrow}
        self.dims = [("wide", s) for s in strides(wide)] + [("narrow", s) for s in strides(narrow)]
        self.core, self.y, self.x = ("wide", 1), ("wide", 2), ("narrow", 1)
        self.rest = [d for d in self.dims if d not in (self.core, self.y, self.x)]

    def bit(self, dim):
        return (lax.axis_index(dim[0]) // dim[1]) % 2

    def swap(self, value, dim):
        axis, stride = dim
        return lax.ppermute(value, axis, [(i, i ^ stride) for i in range(self.size[axis])])

    def open(self, value):
        return value.reshape((1,) * len(self.dims) + value.shape)

    def join(self, value, got, dim):
        low = self.bit(dim) == 0
        return jnp.concatenate(
            [jnp.where(low, value, got), jnp.where(low, got, value)], axis=self.dims.index(dim)
        )

    def grow(self, value, *dims):
        for dim in dims:
            value = self.join(value, self.swap(value, dim), dim)
        return value

    def add(self, mine, got):
        return (mine.astype(F32) + got.astype(F32)).astype(mine.dtype)

    def split(self, value, dim):
        axis, bit = self.dims.index(dim), self.bit(dim)
        return (
            lax.dynamic_index_in_dim(value, bit, axis),
            lax.dynamic_index_in_dim(value, 1 - bit, axis),
        )

    def shrink(self, value, *dims):
        for dim in dims:
            mine, theirs = self.split(value, dim)
            value = self.add(mine, self.swap(theirs, dim))
        return value

    def phase(self, *items):
        parts = [self.split(value, dim) for value, dim in items]
        sends = lax.optimization_barrier([p[1] for p in parts])
        gots = [self.swap(send, dim) for send, (_, dim) in zip(sends, items)]
        gots = lax.optimization_barrier(gots)
        return [self.add(p[0], got) for p, got in zip(parts, gots)]

    def spread(self, value):
        return value.reshape((2,) * len(self.dims) + (-1, value.shape[-1]))

    def halves(self, value):
        mine, theirs = self.split(value, self.core)
        got = self.swap(theirs, self.core)
        low = self.bit(self.core) == 0
        width = value.shape[-1]
        return (
            jnp.where(low, mine, got).reshape(-1, width),
            jnp.where(low, got, mine).reshape(-1, width),
        )


def lanes_of(vec, own, groups):
    n = vec.shape[-1]
    height = -(-n // 128)
    vec = jnp.pad(vec.reshape(groups, n), ((0, 0), (0, height * 128 - n)))
    vec = vec.reshape(groups, height, 128)
    return jnp.pad(vec, ((0, 0), (0, own - height), (0, 0))).reshape(groups * own, 128)


def lanes_back(block, own, groups, n):
    height = -(-n // 128)
    return block.reshape(groups, own, 128)[:, :height].reshape(groups, height * 128)[:, :n]


def per_device(
    sizes, tokens, init_memory, w_query, w_key, w_value, w_output, w_inner, w_outer, vectors,
    chain_start, true_count, cotangent,
):
    cube = Cube(*sizes)
    core = cube.bit(cube.core).reshape(1)
    slots = chain_start.shape[0]
    parts = D * D // w_query.shape[0]
    own = D // parts
    n_vec = vectors.shape[0]
    square = [w.reshape(own, D) for w in (w_query, w_key, w_value, w_output)]
    wqk = cube.open(jnp.concatenate(square[:2], axis=1))
    wvo = cube.open(jnp.concatenate(square[2:] + [lanes_of(vectors, own, 1)], axis=1))
    wi = cube.open(w_inner.reshape(own, FF))
    wu = cube.open(w_outer.reshape(FF // parts, D))
    wqk, wvo = cube.grow(wqk, *cube.rest), cube.grow(wvo, *cube.rest)
    wi, wu = cube.grow(after(wi, wqk), *cube.rest), cube.grow(after(wu, wvo), *cube.rest)
    wqk, wvo = cube.grow(wqk, cube.y, cube.x), cube.grow(wvo, cube.x, cube.y)
    wi, wu = cube.grow(after(wi, wqk), cube.y), cube.grow(after(wu, wvo), cube.x)
    wqk, wvo = cube.grow(wqk, cube.core), cube.grow(wvo, cube.core)
    wqk, wvo = after(wqk, wi), after(wvo, wu)
    wqk, wvo = wqk.reshape(D, -1), wvo.reshape(D, -1)
    wi_got, wu_got = cube.swap(wi, cube.x), cube.swap(wu, cube.y)
    vec_all = lanes_back(wvo[:, 2 * D :], own, parts, n_vec).reshape(-1).astype(F32)
    vecs = vec_all[: 8 * D].reshape(8, D)
    bi = vec_all[8 * D :].reshape(1, FF)

    init = jnp.pad(init_memory.astype(F32), ((0, 0), (0, MPAD - MEM), (0, 0)))
    carry = jnp.zeros((MPAD, D), F32)
    saved = []
    hb = o = h1b = g = mixed = None
    for s in range(slots):
        count = true_count[s : s + 1]
        memory = jnp.where(chain_start[s] > 0, init[s], carry)
        prev = [hb, o] if s else []
        hb, q, k, v, o, linv, e, xhat, rstd = attn_fwd(
            s, slots, prev, count, tokens, memory, wqk, wvo, vecs
        )
        if s == 0:
            wi = cube.join(wi, after(wi_got, xhat), cube.x)
            wu = cube.join(wu, after(wu_got, xhat), cube.y)
            wi = cube.grow(wi, cube.core).reshape(D, FF)
            wu = cube.grow(wu, cube.core).reshape(FF, D)
        prev = [h1b, g, mixed] if s else []
        h1b, g, gp, mixed, carry, xhat2, rstd2 = ffn_fwd(
            s, slots, prev, count, xhat, wi, bi, wu, vecs
        )
        saved.append((q, k, v, linv, e, xhat, rstd, gp, xhat2, rstd2))
    back = jnp.zeros((MPAD, D), F32)
    df2 = df1 = da = dq = dk = dv = grad_tokens = None
    grad_init, vec_parts = [None] * slots, []
    for s in reversed(range(slots)):
        count = true_count[s : s + 1]
        q, k, v, linv, e, xhat, rstd, gp, xhat2, rstd2 = saved[s]
        prev = [df2, df1, da] if df2 is not None else []
        df2, df1, dr1, da, dbi, dvec = ffn_bwd(
            s, slots, prev, count, cotangent, back, xhat2, rstd2, xhat, rstd, wi, wu, gp, vecs
        )
        if s == 0:
            outer = wgrad_outer(core, g, df2)
            inner = wgrad_inner(core, after(h1b, outer), df1)
            outer = cube.spread(cube.add(outer[0], cube.swap(outer[1], cube.core)))
            inner = cube.spread(cube.add(inner[0], cube.swap(inner[1], cube.core)))
            inner, inner_send = cube.split(inner, cube.x)
            outer, outer_send = cube.split(outer, cube.y)
            dr1 = after(dr1, inner_send, outer_send)
            inner_got = cube.swap(inner_send, cube.x)
            outer_got = cube.swap(outer_send, cube.y)
        prev = [dq, dk, dv, grad_tokens] if dq is not None else []
        dq, dk, dv, dqb, dvb, grad_tokens, gmem = attn_bwd(
            s, slots, prev, count, dr1, da, wqk, wvo, q, k, v, o, linv, e
        )
        starts = chain_start[s] > 0
        grad_init[s] = jnp.where(starts, gmem, 0.0)[:MEM]
        back = jnp.where(starts, 0.0, gmem)
        vec_parts.append(
            jnp.concatenate([dqb, dvb, dvec[2:8].reshape(1, -1), dbi], axis=1)
        )
    inner = cube.add(inner, after(inner_got, dq))
    outer = cube.add(outer, after(outer_got, dq))
    inner, inner_send = cube.split(inner, cube.y)
    outer, outer_send = cube.split(outer, cube.x)
    attn = wgrad_attn(core, after(hb, inner_send, outer_send), o, dq, dk, dv, da)
    inner_got = cube.swap(inner_send, cube.y)
    outer_got = cube.swap(outer_send, cube.x)
    inner = cube.add(inner, after(inner_got, attn))
    outer = cube.add(outer, after(outer_got, attn))
    first_got, second_got = cube.swap(attn[1], cube.core), cube.swap(attn[3], cube.core)
    first = cube.spread(cube.add(attn[0], first_got))
    second = cube.spread(cube.add(attn[2], second_got))
    vec = sum(vec_parts).reshape((2,) * len(cube.dims) + (1, n_vec))
    order = cube.rest[::-1]
    first, second, inner, outer, vec = cube.phase(
        (first, cube.x), (second, cube.y), (inner, order[0]), (outer, order[0]), (vec, cube.core)
    )
    first, second, vec = cube.phase((first, cube.y), (second, cube.x), (vec, cube.x))
    inner, outer = cube.shrink(inner, *order[1:]), cube.shrink(outer, *order[1:])
    first, second, vec = cube.phase((first, order[0]), (second, order[0]), (vec, cube.y))
    first, second = cube.shrink(first, *order[1:]), cube.shrink(second, *order[1:])
    vec = cube.shrink(vec, *order)
    g_query, g_value = cube.halves(first)
    g_key, g_output = cube.halves(second)
    inner = jnp.concatenate(cube.halves(inner), axis=1)
    outer = jnp.concatenate(cube.halves(outer), axis=1)
    return (
        mixed,
        grad_tokens,
        jnp.stack(grad_init),
        *(
            piece.astype(F32).reshape(-1)
            for piece in (g_query, g_key, g_value, g_output, inner, outer, vec)
        ),
    )


AXES = ("wide", "narrow")


def solution(mesh):
    flat = P(AXES)
    sizes = (mesh.shape["wide"], mesh.shape["narrow"])
    return jax.shard_map(
        functools.partial(per_device, sizes),
        mesh=mesh,
        in_specs=(P(AXES, None), P(AXES, None, None)) + (flat,) * 9 + (P(AXES, None),),
        out_specs=(P(AXES, None), P(AXES, None), P(AXES, None, None)) + (flat,) * 7,
        check_vma=False,
    )
```

```python
import functools
import math

import jax
import jax.numpy as jnp
from jax import lax
from jax.experimental import pallas as pl
from jax.experimental.pallas import tpu as pltpu
from jax.sharding import PartitionSpec as P

D = 768
HEADS = 12
HEAD_DIM = 64
FF = 3072
SEG = 512
MEM = 10
EPS = 1e-06

MPAD = 16
R = SEG + MPAD
KEYS = 640
QUAD = 256
NQ = D // QUAD
BF = 512
NF = FF // BF
NEG = -1e30
EXP_SCALE = math.log2(math.e) / math.sqrt(HEAD_DIM)
F32 = jnp.float32
BF16 = jnp.bfloat16
VMEM_LIMIT = 60 * 1024 * 1024
MID_LIMIT = 63 * 1024 * 1024


def nt(a, b):
    return lax.dot_general(a, b, (((1,), (1,)), ((), ())), preferred_element_type=F32)


def tn(a, b):
    return lax.dot_general(a, b, (((0,), (0,)), ((), ())), preferred_element_type=F32)


def nn(a, b):
    return jnp.dot(a, b, preferred_element_type=F32)


def col_sum(v):
    return jnp.sum(v, axis=0, keepdims=True)


def row_mean(v):
    return jnp.mean(v, axis=-1, keepdims=True)


def row_ids(rows, cols):
    return lax.broadcasted_iota(jnp.int32, (rows, cols), 0)


def attn_fwd_kernel(
    count_ref, tok_ref, mem_ref, wq_ref, wk_ref, wv_ref, wo_ref, vq_ref, vec_ref,
    hb_ref, q_ref, k_ref, v_ref, o_ref, linv_ref, e_ref, xhat_ref, rstd_ref,
    h_s, k_s, v_s, acc_s,
):
    step = pl.program_id(0)
    count = count_ref[0]

    @pl.when(step == 0)
    def _():
        live = row_ids(SEG, D) < count
        h_s[0:SEG, :] = jnp.where(live, tok_ref[...].astype(F32), 0.0)
        h_s[SEG:R, :] = mem_ref[...]
        hb_ref[...] = h_s[...].astype(BF16)
        k_s[R:KEYS, :] = jnp.zeros((KEYS - R, QUAD), BF16)
        v_s[R:KEYS, :] = jnp.zeros((KEYS - R, QUAD), BF16)

    hb = hb_ref[...]
    q4 = (nn(hb, wq_ref[...]) + vq_ref[0:1, :]).astype(BF16)
    k4 = nn(hb, wk_ref[...]).astype(BF16)
    v4 = (nn(hb, wv_ref[...]) + vq_ref[1:2, :]).astype(BF16)
    q_ref[...] = q4
    k_ref[...] = k4
    v_ref[...] = v4
    k_s[0:R, :] = k4
    v_s[0:R, :] = v4
    key = lax.broadcasted_iota(jnp.int32, (1, KEYS), 1)
    bias = jnp.where(key < count, 0.0, NEG)
    twice = math.log(2.0) * math.sqrt(HEAD_DIM)
    bias = jnp.where((key >= SEG) & (key < SEG + MEM), twice, bias)
    first = lax.broadcasted_iota(jnp.int32, (1, 128), 1) < HEAD_DIM
    one = jnp.ones((KEYS, 128), BF16)
    for pair in range(2):
        lanes = slice(128 * pair, 128 * pair + 128)
        q2 = q4[:, lanes]
        k2 = k_s[:, lanes]
        vx = jnp.concatenate([v_s[:, lanes], one], axis=1)
        outs = []
        for half in range(2):
            mine = first if half == 0 else jnp.logical_not(first)
            qh = jnp.where(mine, q2, jnp.zeros_like(q2))
            s = nt(qh, k2) + bias
            top = jnp.max(s, axis=-1, keepdims=True)
            e = jnp.exp2((s - top) * EXP_SCALE).astype(BF16)
            e_ref[2 * pair + half] = e
            outs.append(nn(e, vx))
        num = jnp.where(first, outs[0][:, :128], outs[1][:, :128])
        den = jnp.where(first, outs[0][:, 128:], outs[1][:, 128:])
        inv = 1.0 / den
        linv_ref[:, lanes] = inv
        o_ref[:, lanes] = (num * inv).astype(BF16)
    part = nn(o_ref[...], wo_ref[...])

    @pl.when(step == 0)
    def _():
        acc_s[...] = part

    @pl.when(step > 0)
    def _():
        acc_s[...] = acc_s[...] + part

    @pl.when(step == NQ - 1)
    def _():
        r = h_s[...] + (acc_s[...] + vec_ref[2:3, :])
        c = r - row_mean(r)
        rstd = lax.rsqrt(row_mean(c * c) + EPS)
        xhat_ref[...] = c * rstd
        rstd_ref[...] = jnp.broadcast_to(rstd, (R, 128))


def const(shape):
    return pl.BlockSpec(shape, lambda j, *_: (0,) * len(shape))


def cols(rows, width):
    return pl.BlockSpec((rows, width), lambda j, *_: (0, j))


def rows(height, width):
    return pl.BlockSpec((height, width), lambda j, *_: (j, 0))


def slot_const(slot):
    return pl.BlockSpec((R, D), lambda j, *_: (slot, 0))


def slot_cols(slot, width):
    return pl.BlockSpec((R, width), lambda j, *_: (slot, j))


def any_spec():
    return pl.BlockSpec(memory_space=pl.ANY)


def sds(shape, dtype):
    return jax.ShapeDtypeStruct(shape, dtype)


def kept(n, kernel):
    def body(*refs):
        return kernel(*refs[:1], *refs[1 + n :])

    return body


def cost(flops, moved):
    return pl.CostEstimate(flops=flops, bytes_accessed=moved, transcendentals=0)


def params():
    return pltpu.CompilerParams(
        dimension_semantics=("arbitrary",), vmem_limit_bytes=VMEM_LIMIT
    )


def attn_fwd(slot, slots, prev, count, tok, mem, wqk, wvo, vecs):
    n = len(prev)
    return pl.pallas_call(
        kept(n, attn_fwd_kernel),
        grid_spec=pltpu.PrefetchScalarGridSpec(
            num_scalar_prefetch=1,
            grid=(NQ,),
            in_specs=[any_spec()] * n + [
                pl.BlockSpec((SEG, D), lambda j, *_: (slot, 0)), const((MPAD, D)),
                cols(D, QUAD), pl.BlockSpec((D, QUAD), lambda j, *_: (0, NQ + j)),
                cols(D, QUAD), pl.BlockSpec((QUAD, D), lambda j, *_: (j, 1)),
                cols(8, QUAD), const((8, D)),
            ],
            out_specs=[
                slot_const(slot), cols(R, QUAD), cols(R, QUAD), cols(R, QUAD),
                slot_cols(slot, QUAD),
                cols(R, QUAD),
                pl.BlockSpec((4, R, KEYS), lambda j, *_: (j, 0, 0)),
                const((R, D)), const((R, 128)),
            ],
            scratch_shapes=[
                pltpu.VMEM((R, D), F32), pltpu.VMEM((KEYS, QUAD), BF16),
                pltpu.VMEM((KEYS, QUAD), BF16), pltpu.VMEM((R, D), F32),
            ],
        ),
        out_shape=[
            sds((slots * R, D), BF16), sds((R, D), BF16), sds((R, D), BF16), sds((R, D), BF16),
            sds((slots * R, D), BF16), sds((R, D), F32), sds((HEADS, R, KEYS), BF16),
            sds((R, D), F32), sds((R, 128), F32),
        ],
        input_output_aliases={1: 0, 2: 4} if n else {},
        compiler_params=params(),
        cost_estimate=cost(2 * R * (4 * D * D + 2 * KEYS * D * 4), 20_000_000),
        name="attn_fwd",
    )(count, *prev, tok, mem, wqk, wqk, wvo, wvo, vecs, vecs)


def norm_pull(grad, gain, xhat, rstd):
    gx = grad * gain
    return rstd * (gx - row_mean(gx) - xhat * row_mean(gx * xhat))


def attn_bwd_kernel(
    count_ref, dr1_ref, dr1b_ref, wq_ref, wk_ref, wv_ref, wo_ref, q_ref, k_ref, v_ref, o_ref,
    linv_ref, e_ref,
    dq_ref, dk_ref, dv_ref, dqb_ref, dvb_ref, gtok_ref, gmem_ref,
    k_s, v_s, acc_s,
):
    step = pl.program_id(0)

    @pl.when(step == 0)
    def _():
        k_s[R:KEYS, :] = jnp.zeros((KEYS - R, QUAD), BF16)
        v_s[R:KEYS, :] = jnp.zeros((KEYS - R, QUAD), BF16)
        acc_s[...] = dr1_ref[...]

    k_s[0:R, :] = k_ref[...]
    v_s[0:R, :] = v_ref[...]
    grad_o = nt(dr1b_ref[...], wo_ref[...]).astype(BF16).astype(F32) * linv_ref[...]
    grad_ob = grad_o.astype(BF16)
    term = (-(grad_o * o_ref[...].astype(F32))).astype(BF16)
    first = lax.broadcasted_iota(jnp.int32, (1, 128), 1) < HEAD_DIM
    one = jnp.ones((KEYS, 128), BF16)
    scaling = 1.0 / math.sqrt(HEAD_DIM)
    for pair in range(2):
        lanes = slice(128 * pair, 128 * pair + 128)
        q2 = q_ref[:, lanes]
        k2 = k_s[:, lanes]
        do2 = grad_ob[:, lanes]
        tm2 = term[:, lanes]
        vx = jnp.concatenate([v_s[:, lanes], one], axis=1)
        dqs, dks, dvs = [], [], []
        for half in range(2):
            mine = first if half == 0 else jnp.logical_not(first)
            zero = jnp.zeros_like(do2)
            lhs = jnp.concatenate([jnp.where(mine, do2, zero), jnp.where(mine, tm2, zero)], axis=1)
            e = e_ref[2 * pair + half]
            ds = (nt(lhs, vx) * e.astype(F32)).astype(BF16)
            dqs.append(nn(ds, k2))
            dks.append(tn(ds, q2))
            dvs.append(tn(e, do2))
        dq_ref[:, lanes] = (jnp.where(first, dqs[0], dqs[1]) * scaling).astype(BF16)
        dk_ref[:, lanes] = (jnp.where(first, dks[0], dks[1])[0:R, :] * scaling).astype(BF16)
        dv_ref[:, lanes] = jnp.where(first, dvs[0], dvs[1])[0:R, :].astype(BF16)
    dq = dq_ref[...]
    dv = dv_ref[...]
    dqb_ref[...] = col_sum(dq.astype(F32))
    dvb_ref[...] = col_sum(dv.astype(F32))
    part = nt(dq, wq_ref[...]) + nt(dk_ref[...], wk_ref[...]) + nt(dv, wv_ref[...])
    acc_s[...] = acc_s[...] + part

    @pl.when(step == NQ - 1)
    def _():
        live = row_ids(SEG, D) < count_ref[0]
        gtok_ref[...] = jnp.where(live, acc_s[0:SEG, :], 0.0)
        gmem_ref[...] = jnp.where(row_ids(MPAD, D) < MEM, acc_s[SEG:R, :], 0.0)


def attn_bwd(slot, slots, prev, count, dr1, dr1b, wqk, wvo, q, k, v, o, linv, e):
    n = len(prev)
    return pl.pallas_call(
        kept(n, attn_bwd_kernel),
        grid_spec=pltpu.PrefetchScalarGridSpec(
            num_scalar_prefetch=1,
            grid=(NQ,),
            in_specs=[any_spec()] * n + [
                const((R, D)), slot_const(slot),
                cols(D, QUAD), pl.BlockSpec((D, QUAD), lambda j, *_: (0, NQ + j)),
                cols(D, QUAD), pl.BlockSpec((QUAD, D), lambda j, *_: (j, 1)),
                cols(R, QUAD), cols(R, QUAD), cols(R, QUAD), slot_cols(slot, QUAD),
                cols(R, QUAD),
                pl.BlockSpec((4, R, KEYS), lambda j, *_: (j, 0, 0)),
            ],
            out_specs=[
                slot_cols(slot, QUAD), slot_cols(slot, QUAD), slot_cols(slot, QUAD),
                cols(1, QUAD), cols(1, QUAD),
                pl.BlockSpec((SEG, D), lambda j, *_: (slot, 0)), const((MPAD, D)),
            ],
            scratch_shapes=[
                pltpu.VMEM((KEYS, QUAD), BF16), pltpu.VMEM((KEYS, QUAD), BF16),
                pltpu.VMEM((R, D), F32),
            ],
        ),
        out_shape=[
            sds((slots * R, D), BF16), sds((slots * R, D), BF16), sds((slots * R, D), BF16),
            sds((1, D), F32), sds((1, D), F32), sds((slots * SEG, D), F32), sds((MPAD, D), F32),
        ],
        input_output_aliases={1: 0, 2: 1, 3: 2, 4: 5} if n else {},
        compiler_params=params(),
        cost_estimate=cost(2 * R * (4 * D * D + 5 * KEYS * D * 4), 20_000_000),
        name="attn_bwd",
    )(count, *prev, dr1, dr1b, wqk, wqk, wvo, wvo, q, k, v, o, linv, e)


MID_BF = 512


def mid_kernel(
    info_ref, xhat0_ref, rstd0_ref, init_ref, vec_ref, bi_ref,
    wqk_hbm, wvo_hbm, wi_hbm, wu_hbm, tok_hbm, cot_hbm, hb_in, o_in,
    mixed_hbm, hb_hbm, o_hbm, h1b_hbm, g_hbm, df2_hbm, df1_hbm, da_hbm,
    dq_hbm, dk_hbm, dv_hbm, gtok_hbm, dr1_hbm, gmem_ref, dvec_ref, dbi_ref,
    wqk_s, wvo_s, wi_s, wu_s, gp_s, g_s, xhat_s, xhat2_s, rstd_s, rstd2_s, h1b_s,
    hb_s, q_s, k_s, v_s, o_s, linv_s, e_s, h_s, acc_s, df2_s, da_s, tok_s, cot_s, mixed_s, mem_s,
    sems,
):
    used = [0]

    def copy(src, dst):
        used[0] += 1
        return pltpu.make_async_copy(src, dst, sems.at[used[0] - 1])

    half = FF // 2
    in_wi = [
        copy(wi_hbm.at[:, half * i : half * i + half], wi_s.at[:, half * i : half * i + half])
        for i in range(2)
    ]
    in_wu = [
        copy(wu_hbm.at[half * i : half * i + half], wu_s.at[half * i : half * i + half])
        for i in range(2)
    ]
    in_tok = copy(tok_hbm.at[SEG : 2 * SEG], tok_s)
    in_wqk = copy(wqk_hbm, wqk_s)
    in_wvo = copy(wvo_hbm.at[:, 0 : 2 * D], wvo_s)
    in_cot1 = copy(cot_hbm.at[SEG : 2 * SEG], cot_s)
    for c in (in_wi[0], in_wu[0], in_wi[1], in_wu[1], in_tok, in_wqk, in_wvo, in_cot1):
        c.start()
    xhat_s[0] = xhat0_ref[...]
    rstd_s[0] = rstd0_ref[...]
    k_s[R:KEYS, :] = jnp.zeros((KEYS - R, D), BF16)
    v_s[R:KEYS, :] = jnp.zeros((KEYS - R, D), BF16)
    first = lax.broadcasted_iota(jnp.int32, (1, 128), 1) < HEAD_DIM
    one = jnp.ones((KEYS, 128), BF16)

    def row(i):
        return vec_ref[i : i + 1, :]

    def lanes(start, size):
        return pl.ds(pl.multiple_of(start, size), size)

    def feed_forward(seg):
        h1 = xhat_s[seg] * row(3) + row(4)
        h1b_s[...] = h1.astype(BF16)
        acc_s[...] = h1 + row(5)

        def chunk(j, carry):
            at = lanes(j * MID_BF, MID_BF)
            f1 = nn(h1b_s[...], wi_s[:, at]) + bi_ref[:, at]
            cdf = 0.5 * (1.0 + lax.erf(f1 * math.sqrt(0.5)))
            pdf = jnp.exp(-0.5 * f1 * f1) * (1.0 / math.sqrt(2.0 * math.pi))
            g = (f1 * cdf).astype(BF16)
            g_s[:, at] = g
            gp_s[seg, :, at] = (cdf + f1 * pdf).astype(BF16)
            acc_s[...] = acc_s[...] + nn(g, wu_s[at, :])
            return carry

        n = half // MID_BF
        if seg == 0:
            in_wi[0].wait()
            in_wu[0].wait()
        lax.fori_loop(0, n, chunk, 0)
        if seg == 0:
            in_wi[1].wait()
            in_wu[1].wait()
        lax.fori_loop(n, 2 * n, chunk, 0)
        r = acc_s[...]
        c = r - row_mean(r)
        rstd = lax.rsqrt(row_mean(c * c) + EPS)
        xhat = c * rstd
        xhat2_s[seg] = xhat
        rstd2_s[seg] = jnp.broadcast_to(rstd, (R, 128))
        y = xhat * row(6) + row(7)
        live = row_ids(SEG, D) < info_ref[seg]
        mixed_s[...] = jnp.where(live, y[0:SEG, :], 0.0).astype(BF16)
        if seg == 0:
            write = jnp.where(row_ids(MPAD, D) < MEM, y[SEG:R, :], 0.0)
            mem_s[...] = jnp.where(info_ref[2] > 0, init_ref[...], write)

    def feed_forward_back(seg, grad_write):
        live = row_ids(SEG, D) < info_ref[seg]
        acc_s[0:SEG, :] = jnp.where(live, cot_s[...].astype(F32), 0.0)
        acc_s[SEG:R, :] = grad_write
        dy = acc_s[...]
        xhat2 = xhat2_s[seg]
        sums = [col_sum(dy * xhat2), col_sum(dy)]
        dr2 = norm_pull(dy, row(6), xhat2, rstd2_s[seg, :, 0:1])
        df2 = dr2.astype(BF16)
        df2_s[...] = df2
        sums.insert(0, col_sum(df2.astype(F32)))
        acc_s[...] = dr2

        def chunk(j, carry):
            at = lanes(j * MID_BF, MID_BF)
            df1 = (nt(df2_s[...], wu_s[at, :]) * gp_s[seg, :, at].astype(F32)).astype(BF16)
            gp_s[seg, :, at] = df1
            total = col_sum(df1.astype(F32))
            dbi_ref[:, at] = total if seg == 1 else dbi_ref[:, at] + total
            acc_s[...] = acc_s[...] + nt(df1, wi_s[:, at])
            return carry

        lax.fori_loop(0, FF // MID_BF, chunk, 0)
        dh1 = acc_s[...]
        xhat = xhat_s[seg]
        sums = [col_sum(dh1 * xhat), col_sum(dh1)] + sums
        dr1 = norm_pull(dh1, row(3), xhat, rstd_s[seg, :, 0:1])
        acc_s[...] = dr1
        da = dr1.astype(BF16)
        da_s[...] = da
        sums = [col_sum(da.astype(F32))] + sums
        for i, total in enumerate(sums):
            at = slice(2 + i, 3 + i)
            dvec_ref[at, :] = total if seg == 1 else dvec_ref[at, :] + total

    feed_forward(0)
    outs = {}

    def send(name, src, dst):
        outs[name] = copy(src, dst)
        outs[name].start()

    def done(*names):
        for name in names:
            outs.pop(name).wait()

    send("h1b0", h1b_s, h1b_hbm.at[0:R])
    send("g0", g_s, g_hbm.at[0:R])
    send("mixed0", mixed_s, mixed_hbm.at[0:SEG])

    in_tok.wait()
    live = row_ids(SEG, D) < info_ref[1]
    h_s[0:SEG, :] = jnp.where(live, tok_s[...].astype(F32), 0.0)
    h_s[SEG:R, :] = mem_s[...]
    hb_s[...] = h_s[...].astype(BF16)
    send("hb", hb_s, hb_hbm.at[R : 2 * R])
    in_wqk.wait()
    in_wvo.wait()
    acc_s[...] = h_s[...] + row(2)
    key = lax.broadcasted_iota(jnp.int32, (1, KEYS), 1)
    bias = jnp.where(key < info_ref[1], 0.0, NEG)
    twice = math.log(2.0) * math.sqrt(HEAD_DIM)
    bias = jnp.where((key >= SEG) & (key < SEG + MEM), twice, bias)

    def quad_forward(j, carry):
        at = lanes(j * QUAD, QUAD)
        hb = hb_s[...]
        q_s[:, at] = (nn(hb, wqk_s[:, at]) + vec_ref[0:1, at]).astype(BF16)
        k_s[0:R, at] = nn(hb, wqk_s[:, lanes(D + j * QUAD, QUAD)]).astype(BF16)
        v_s[0:R, at] = (nn(hb, wvo_s[:, at]) + vec_ref[1:2, at]).astype(BF16)
        for pair in range(2):
            here = lanes(j * QUAD + 128 * pair, 128)
            q2 = q_s[:, here]
            k2 = k_s[:, here]
            vx = jnp.concatenate([v_s[:, here], one], axis=1)
            parts = []
            for side in range(2):
                mine = first if side == 0 else jnp.logical_not(first)
                s = nt(jnp.where(mine, q2, jnp.zeros_like(q2)), k2) + bias
                top = jnp.max(s, axis=-1, keepdims=True)
                e = jnp.exp2((s - top) * EXP_SCALE).astype(BF16)
                e_s[4 * j + 2 * pair + side] = e
                parts.append(nn(e, vx))
            num = jnp.where(first, parts[0][:, :128], parts[1][:, :128])
            den = jnp.where(first, parts[0][:, 128:], parts[1][:, 128:])
            inv = 1.0 / den
            linv_s[:, here] = inv
            o_s[:, here] = (num * inv).astype(BF16)
        acc_s[...] = acc_s[...] + nn(o_s[:, at], wvo_s[at, D : 2 * D])
        return carry

    lax.fori_loop(0, NQ, quad_forward, 0)
    send("o", o_s, o_hbm.at[R : 2 * R])
    r = acc_s[...]
    c = r - row_mean(r)
    rstd = lax.rsqrt(row_mean(c * c) + EPS)
    xhat_s[1] = c * rstd
    rstd_s[1] = jnp.broadcast_to(rstd, (R, 128))

    done("h1b0", "g0", "mixed0")
    feed_forward(1)
    send("h1b1", h1b_s, h1b_hbm.at[R : 2 * R])
    send("g1", g_s, g_hbm.at[R : 2 * R])
    send("mixed1", mixed_s, mixed_hbm.at[SEG : 2 * SEG])

    in_cot1.wait()
    feed_forward_back(1, jnp.zeros((MPAD, D), F32))
    in_cot0 = copy(cot_hbm.at[0:SEG], cot_s)
    in_cot0.start()
    send("df2", df2_s, df2_hbm.at[R : 2 * R])
    send("df1", gp_s.at[1], df1_hbm.at[R : 2 * R])
    send("da", da_s, da_hbm.at[R : 2 * R])

    scaling = 1.0 / math.sqrt(HEAD_DIM)
    done("hb", "o")

    def quad_back(j, carry):
        at = lanes(j * QUAD, QUAD)
        grad_o = nt(da_s[...], wvo_s[at, D : 2 * D]).astype(BF16).astype(F32) * linv_s[:, at]
        grad_ob = grad_o.astype(BF16)
        term = (-(grad_o * o_s[:, at].astype(F32))).astype(BF16)
        for pair in range(2):
            here = lanes(j * QUAD + 128 * pair, 128)
            part = slice(128 * pair, 128 * pair + 128)
            q2 = q_s[:, here]
            k2 = k_s[:, here]
            do2 = grad_ob[:, part]
            tm2 = term[:, part]
            vx = jnp.concatenate([v_s[:, here], one], axis=1)
            dqs, dks, dvs = [], [], []
            for side in range(2):
                mine = first if side == 0 else jnp.logical_not(first)
                zero = jnp.zeros_like(do2)
                lhs = jnp.concatenate(
                    [jnp.where(mine, do2, zero), jnp.where(mine, tm2, zero)], axis=1
                )
                e = e_s[4 * j + 2 * pair + side]
                ds = (nt(lhs, vx) * e.astype(F32)).astype(BF16)
                dqs.append(nn(ds, k2))
                dks.append(tn(ds, q2))
                dvs.append(tn(e, do2))
            q_s[:, here] = (jnp.where(first, dqs[0], dqs[1]) * scaling).astype(BF16)
            k_s[0:R, here] = (jnp.where(first, dks[0], dks[1])[0:R, :] * scaling).astype(BF16)
            v_s[0:R, here] = jnp.where(first, dvs[0], dvs[1])[0:R, :].astype(BF16)
        dq = q_s[:, at]
        dk = k_s[0:R, at]
        dv = v_s[0:R, at]
        dvec_ref[0:1, at] = col_sum(dq.astype(F32))
        dvec_ref[1:2, at] = col_sum(dv.astype(F32))
        part = nt(dq, wqk_s[:, at]) + nt(dk, wqk_s[:, lanes(D + j * QUAD, QUAD)])
        acc_s[...] = acc_s[...] + (part + nt(dv, wvo_s[:, at]))
        return carry

    lax.fori_loop(0, NQ, quad_back, 0)
    send("dq", q_s, dq_hbm.at[R : 2 * R])
    send("dk", k_s.at[0:R], dk_hbm.at[R : 2 * R])
    send("dv", v_s.at[0:R], dv_hbm.at[R : 2 * R])
    h_s[0:SEG, :] = jnp.where(live, acc_s[0:SEG, :], 0.0)
    send("gtok", h_s.at[0:SEG], gtok_hbm.at[SEG : 2 * SEG])
    grad_mem = jnp.where(row_ids(MPAD, D) < MEM, acc_s[SEG:R, :], 0.0)
    gmem_ref[...] = grad_mem
    in_cot0.wait()
    done("df2", "da")
    feed_forward_back(0, jnp.where(info_ref[2] > 0, 0.0, grad_mem))
    send("df2", df2_s, df2_hbm.at[0:R])
    send("df1b", gp_s.at[0], df1_hbm.at[0:R])
    send("da", da_s, da_hbm.at[0:R])
    send("dr1", acc_s, dr1_hbm)
    done(*list(outs))


def mid(info, xhat0, rstd0, init, vecs, bi, wqk, wvo, wi, wu, tok, cot, hb, o):
    whole = pl.BlockSpec(memory_space=pltpu.VMEM)
    smem = pl.BlockSpec(memory_space=pltpu.SMEM)
    two = 2 * R
    return pl.pallas_call(
        mid_kernel,
        in_specs=[smem] + [whole] * 5 + [any_spec()] * 8,
        out_specs=[any_spec()] * 13 + [whole] * 3,
        out_shape=[
            sds((2 * SEG, D), BF16), sds((two, D), BF16), sds((two, D), BF16),
            sds((two, D), BF16), sds((two, FF), BF16), sds((two, D), BF16),
            sds((two, FF), BF16), sds((two, D), BF16), sds((two, D), BF16),
            sds((two, D), BF16), sds((two, D), BF16), sds((2 * SEG, D), F32),
            sds((R, D), F32), sds((MPAD, D), F32), sds((8, D), F32), sds((1, FF), F32),
        ],
        scratch_shapes=[
            pltpu.VMEM((D, 2 * D), BF16), pltpu.VMEM((D, 2 * D), BF16),
            pltpu.VMEM((D, FF), BF16), pltpu.VMEM((FF, D), BF16),
            pltpu.VMEM((2, R, FF), BF16), pltpu.VMEM((R, FF), BF16),
            pltpu.VMEM((2, R, D), F32), pltpu.VMEM((2, R, D), F32),
            pltpu.VMEM((2, R, 128), F32), pltpu.VMEM((2, R, 128), F32),
            pltpu.VMEM((R, D), BF16),
            pltpu.VMEM((R, D), BF16), pltpu.VMEM((R, D), BF16), pltpu.VMEM((KEYS, D), BF16),
            pltpu.VMEM((KEYS, D), BF16), pltpu.VMEM((R, D), BF16), pltpu.VMEM((R, D), F32),
            pltpu.VMEM((HEADS, R, KEYS), BF16),
            pltpu.VMEM((R, D), F32), pltpu.VMEM((R, D), F32),
            pltpu.VMEM((R, D), BF16), pltpu.VMEM((R, D), BF16),
            pltpu.VMEM((SEG, D), BF16), pltpu.VMEM((SEG, D), BF16), pltpu.VMEM((SEG, D), BF16),
            pltpu.VMEM((MPAD, D), F32),
            pltpu.SemaphoreType.DMA((32,)),
        ],
        input_output_aliases={12: 1, 13: 2},
        compiler_params=pltpu.CompilerParams(vmem_limit_bytes=MID_LIMIT),
        cost_estimate=cost(2 * R * 40 * D * D + 14 * R * KEYS * D * 4, 60_000_000),
        name="mid",
    )(info, xhat0, rstd0, init, vecs, bi, wqk, wvo, wi, wu, tok, cot, hb, o)


def wgrad_inner_kernel(core_ref, h_ref, da_ref, db_ref, mine_ref, theirs_ref):
    mine_ref[...] = tn(h_ref[...], da_ref[...]).astype(BF16)
    theirs_ref[...] = tn(h_ref[...], db_ref[...]).astype(BF16)


def wgrad_inner(core, h, d):
    depth, n = h.shape[0], FF // D // 2
    return pl.pallas_call(
        wgrad_inner_kernel,
        grid_spec=pltpu.PrefetchScalarGridSpec(
            num_scalar_prefetch=1,
            grid=(n,),
            in_specs=[
                const((depth, D)),
                pl.BlockSpec((depth, D), lambda j, c: (0, c[0] * n + j)),
                pl.BlockSpec((depth, D), lambda j, c: (0, (1 - c[0]) * n + j)),
            ],
            out_specs=[cols(D, D), cols(D, D)],
        ),
        out_shape=[sds((D, FF // 2), BF16)] * 2,
        compiler_params=params(),
        cost_estimate=cost(2 * depth * D * FF * 2, 15_000_000),
        name="wgrad_inner",
    )(core, h, d, d)


def wgrad_outer_kernel(core_ref, g_ref, d_ref, mine_ref, theirs_ref):
    full = tn(g_ref[...], d_ref[...]).astype(BF16)
    low = core_ref[0] == 0
    left, right = full[:, : D // 2], full[:, D // 2 :]
    mine_ref[...] = jnp.where(low, left, right)
    theirs_ref[...] = jnp.where(low, right, left)


def wgrad_outer(core, g, d):
    depth, n = g.shape[0], FF // D
    return pl.pallas_call(
        wgrad_outer_kernel,
        grid_spec=pltpu.PrefetchScalarGridSpec(
            num_scalar_prefetch=1,
            grid=(n,),
            in_specs=[cols(depth, D), const((depth, D))],
            out_specs=[rows(D, D // 2), rows(D, D // 2)],
        ),
        out_shape=[sds((FF, D // 2), BF16)] * 2,
        compiler_params=params(),
        cost_estimate=cost(2 * depth * D * FF * 2, 15_000_000),
        name="wgrad_outer",
    )(core, g, d)


def wgrad_attn_kernel(
    core_ref, hb_ref, o_ref, dq_ref, dk_ref, dv_ref, da_ref, qv_ref, vq_ref, ko_ref, ok_ref
):
    low = core_ref[0] == 0

    def put(mine_ref, theirs_ref, left, right):
        mine_ref[...] = jnp.where(low, left, right)
        theirs_ref[...] = jnp.where(low, right, left)

    dq, dk = tn(hb_ref[...], dq_ref[...]), tn(hb_ref[...], dk_ref[...])
    dv, do = tn(hb_ref[...], dv_ref[...]), tn(o_ref[...], da_ref[...])
    put(qv_ref, vq_ref, dq.astype(BF16), dv.astype(BF16))
    put(ko_ref, ok_ref, dk.astype(BF16), do.astype(BF16))


def wgrad_attn(core, hb, o, dq, dk, dv, da):
    depth, n = hb.shape[0], D // QUAD
    return pl.pallas_call(
        wgrad_attn_kernel,
        grid_spec=pltpu.PrefetchScalarGridSpec(
            num_scalar_prefetch=1,
            grid=(n,),
            in_specs=[const((depth, D))] * 2 + [cols(depth, QUAD)] * 4,
            out_specs=[cols(D, QUAD)] * 4,
        ),
        out_shape=[sds((D, D), BF16)] * 4,
        compiler_params=params(),
        cost_estimate=cost(2 * depth * D * D * 4 * 2, 15_000_000),
        name="wgrad_attn",
    )(core, hb, o, dq, dk, dv, da)


def strides(size):
    return [1 << i for i in reversed(range(size.bit_length() - 1))]


def after(value, *others):
    return lax.optimization_barrier((value, others))[0]


class Cube:
    def __init__(self, wide, narrow):
        self.size = {"wide": wide, "narrow": narrow}
        self.dims = [("wide", s) for s in strides(wide)] + [("narrow", s) for s in strides(narrow)]
        self.core, self.y, self.x = ("wide", 1), ("wide", 2), ("narrow", 1)
        self.rest = [d for d in self.dims if d not in (self.core, self.y, self.x)]

    def bit(self, dim):
        return (lax.axis_index(dim[0]) // dim[1]) % 2

    def swap(self, value, dim):
        axis, stride = dim
        return lax.ppermute(value, axis, [(i, i ^ stride) for i in range(self.size[axis])])

    def open(self, value):
        return value.reshape((1,) * len(self.dims) + value.shape)

    def join(self, value, got, dim):
        low = self.bit(dim) == 0
        return jnp.concatenate(
            [jnp.where(low, value, got), jnp.where(low, got, value)], axis=self.dims.index(dim)
        )

    def grow(self, value, *dims):
        for dim in dims:
            value = self.join(value, self.swap(value, dim), dim)
        return value

    def add(self, mine, got):
        return (mine.astype(F32) + got.astype(F32)).astype(mine.dtype)

    def split(self, value, dim):
        axis, bit = self.dims.index(dim), self.bit(dim)
        return (
            lax.dynamic_index_in_dim(value, bit, axis),
            lax.dynamic_index_in_dim(value, 1 - bit, axis),
        )

    def shrink(self, value, *dims):
        for dim in dims:
            mine, theirs = self.split(value, dim)
            value = self.add(mine, self.swap(theirs, dim))
        return value

    def phase(self, *items):
        parts = [self.split(value, dim) for value, dim in items]
        sends = lax.optimization_barrier([p[1] for p in parts])
        gots = [self.swap(send, dim) for send, (_, dim) in zip(sends, items)]
        gots = lax.optimization_barrier(gots)
        return [self.add(p[0], got) for p, got in zip(parts, gots)]

    def spread(self, value):
        return value.reshape((2,) * len(self.dims) + (-1, value.shape[-1]))

    def halves(self, value):
        mine, theirs = self.split(value, self.core)
        got = self.swap(theirs, self.core)
        low = self.bit(self.core) == 0
        width = value.shape[-1]
        return (
            jnp.where(low, mine, got).reshape(-1, width),
            jnp.where(low, got, mine).reshape(-1, width),
        )


def lanes_of(vec, own, groups):
    n = vec.shape[-1]
    height = -(-n // 128)
    vec = jnp.pad(vec.reshape(groups, n), ((0, 0), (0, height * 128 - n)))
    vec = vec.reshape(groups, height, 128)
    return jnp.pad(vec, ((0, 0), (0, own - height), (0, 0))).reshape(groups * own, 128)


def lanes_back(block, own, groups, n):
    height = -(-n // 128)
    return block.reshape(groups, own, 128)[:, :height].reshape(groups, height * 128)[:, :n]


def per_device(
    sizes, tokens, init_memory, w_query, w_key, w_value, w_output, w_inner, w_outer, vectors,
    chain_start, true_count, cotangent,
):
    cube = Cube(*sizes)
    core = cube.bit(cube.core).reshape(1)
    slots = chain_start.shape[0]
    parts = D * D // w_query.shape[0]
    own = D // parts
    n_vec = vectors.shape[0]
    square = [w.reshape(own, D) for w in (w_query, w_key, w_value, w_output)]
    wqk = cube.open(jnp.concatenate(square[:2], axis=1))
    wvo = cube.open(jnp.concatenate(square[2:] + [lanes_of(vectors, own, 1)], axis=1))
    wi = cube.open(w_inner.reshape(own, FF))
    wu = cube.open(w_outer.reshape(FF // parts, D))
    wqk, wvo = cube.grow(wqk, *cube.rest), cube.grow(wvo, *cube.rest)
    wi, wu = cube.grow(after(wi, wqk), *cube.rest), cube.grow(after(wu, wvo), *cube.rest)
    wqk, wvo = cube.grow(wqk, cube.y, cube.x), cube.grow(wvo, cube.x, cube.y)
    wi, wu = cube.grow(after(wi, wqk), cube.y), cube.grow(after(wu, wvo), cube.x)
    wqk, wvo = cube.grow(wqk, cube.core), cube.grow(wvo, cube.core)
    wqk, wvo = after(wqk, wi), after(wvo, wu)
    wqk, wvo = wqk.reshape(D, -1), wvo.reshape(D, -1)
    wi_got, wu_got = cube.swap(wi, cube.x), cube.swap(wu, cube.y)
    vec_all = lanes_back(wvo[:, 2 * D :], own, parts, n_vec).reshape(-1).astype(F32)
    vecs = vec_all[: 8 * D].reshape(8, D)
    bi = vec_all[8 * D :].reshape(1, FF)

    init = jnp.pad(init_memory.astype(F32), ((0, 0), (0, MPAD - MEM), (0, 0)))
    count = true_count[0:1]
    hb, q, k, v, o, linv, e, xhat, rstd = attn_fwd(
        0, slots, [], count, tokens, init[0], wqk, wvo, vecs
    )
    wi = cube.join(wi, after(wi_got, xhat), cube.x)
    wu = cube.join(wu, after(wu_got, xhat), cube.y)
    wi = cube.grow(wi, cube.core).reshape(D, FF)
    wu = cube.grow(wu, cube.core).reshape(FF, D)
    info = jnp.concatenate([true_count, chain_start[1:2]])
    (
        mixed, hb, o, h1b, g, df2, df1, da, dq, dk, dv, grad_tokens, dr1, gmem, dvec, dbi,
    ) = mid(info, xhat, rstd, init[1], vecs, bi, wqk, wvo, wi, wu, tokens, cotangent, hb, o)
    grad_init = [None, jnp.where(chain_start[1] > 0, gmem, 0.0)[:MEM]]
    outer = wgrad_outer(core, g, df2)
    inner = wgrad_inner(core, after(h1b, outer), df1)
    outer = cube.spread(cube.add(outer[0], cube.swap(outer[1], cube.core)))
    inner = cube.spread(cube.add(inner[0], cube.swap(inner[1], cube.core)))
    inner, inner_send = cube.split(inner, cube.x)
    outer, outer_send = cube.split(outer, cube.y)
    dr1 = after(dr1, inner_send, outer_send)
    inner_got = cube.swap(inner_send, cube.x)
    outer_got = cube.swap(outer_send, cube.y)
    dq, dk, dv, dqb, dvb, grad_tokens, gmem = attn_bwd(
        0, slots, [dq, dk, dv, grad_tokens], count, dr1, da, wqk, wvo, q, k, v, o, linv, e
    )
    grad_init[0] = gmem[:MEM]
    vec_parts = [
        jnp.concatenate([dvec.reshape(1, -1), dbi], axis=1),
        jnp.concatenate([dqb, dvb, jnp.zeros((1, 6 * D + FF), F32)], axis=1),
    ]
    inner = cube.add(inner, after(inner_got, dq))
    outer = cube.add(outer, after(outer_got, dq))
    inner, inner_send = cube.split(inner, cube.y)
    outer, outer_send = cube.split(outer, cube.x)
    attn = wgrad_attn(core, after(hb, inner_send, outer_send), o, dq, dk, dv, da)
    inner_got = cube.swap(inner_send, cube.y)
    outer_got = cube.swap(outer_send, cube.x)
    inner = cube.add(inner, after(inner_got, attn))
    outer = cube.add(outer, after(outer_got, attn))
    first_got, second_got = cube.swap(attn[1], cube.core), cube.swap(attn[3], cube.core)
    first = cube.spread(cube.add(attn[0], first_got))
    second = cube.spread(cube.add(attn[2], second_got))
    vec = sum(vec_parts).reshape((2,) * len(cube.dims) + (1, n_vec))
    order = cube.rest[::-1]
    first, second, inner, outer, vec = cube.phase(
        (first, cube.x), (second, cube.y), (inner, order[0]), (outer, order[0]), (vec, cube.core)
    )
    first, second, vec = cube.phase((first, cube.y), (second, cube.x), (vec, cube.x))
    inner, outer = cube.shrink(inner, *order[1:]), cube.shrink(outer, *order[1:])
    first, second, vec = cube.phase((first, order[0]), (second, order[0]), (vec, cube.y))
    first, second = cube.shrink(first, *order[1:]), cube.shrink(second, *order[1:])
    vec = cube.shrink(vec, *order)
    g_query, g_value = cube.halves(first)
    g_key, g_output = cube.halves(second)
    inner = jnp.concatenate(cube.halves(inner), axis=1)
    outer = jnp.concatenate(cube.halves(outer), axis=1)
    return (
        mixed,
        grad_tokens,
        jnp.stack(grad_init),
        *(
            piece.astype(F32).reshape(-1)
            for piece in (g_query, g_key, g_value, g_output, inner, outer, vec)
        ),
    )


AXES = ("wide", "narrow")


def solution(mesh):
    flat = P(AXES)
    sizes = (mesh.shape["wide"], mesh.shape["narrow"])
    return jax.shard_map(
        functools.partial(per_device, sizes),
        mesh=mesh,
        in_specs=(P(AXES, None), P(AXES, None, None)) + (flat,) * 9 + (P(AXES, None),),
        out_specs=(P(AXES, None), P(AXES, None), P(AXES, None, None)) + (flat,) * 7,
        check_vma=False,
    )
```

```python
import functools
import math

import jax
import jax.numpy as jnp
from jax import lax
from jax.experimental import pallas as pl
from jax.experimental.pallas import tpu as pltpu
from jax.sharding import PartitionSpec as P

D = 768
HEADS = 12
HEAD_DIM = 64
FF = 3072
SEG = 512
MEM = 10
EPS = 1e-06

MPAD = 16
R = SEG + MPAD
KEYS = 640
QUAD = 256
NQ = D // QUAD
BF = 512
NF = FF // BF
NEG = -1e30
EXP_SCALE = math.log2(math.e) / math.sqrt(HEAD_DIM)
F32 = jnp.float32
BF16 = jnp.bfloat16
VMEM_LIMIT = 60 * 1024 * 1024
MID_LIMIT = 63 * 1024 * 1024


def nt(a, b):
    return lax.dot_general(a, b, (((1,), (1,)), ((), ())), preferred_element_type=F32)


def tn(a, b):
    return lax.dot_general(a, b, (((0,), (0,)), ((), ())), preferred_element_type=F32)


def nn(a, b):
    return jnp.dot(a, b, preferred_element_type=F32)


def col_sum(v):
    return jnp.sum(v, axis=0, keepdims=True)


def row_mean(v):
    return jnp.mean(v, axis=-1, keepdims=True)


def row_ids(rows, cols):
    return lax.broadcasted_iota(jnp.int32, (rows, cols), 0)


def attn_fwd_kernel(
    count_ref, tok_ref, mem_ref, wq_ref, wk_ref, wv_ref, wo_ref, vq_ref, vec_ref,
    hb_ref, q_ref, k_ref, v_ref, o_ref, linv_ref, e_ref, xhat_ref, rstd_ref,
    h_s, k_s, v_s, acc_s,
):
    step = pl.program_id(0)
    count = count_ref[0]

    @pl.when(step == 0)
    def _():
        live = row_ids(SEG, D) < count
        h_s[0:SEG, :] = jnp.where(live, tok_ref[...].astype(F32), 0.0)
        h_s[SEG:R, :] = mem_ref[...]
        hb_ref[...] = h_s[...].astype(BF16)
        k_s[R:KEYS, :] = jnp.zeros((KEYS - R, QUAD), BF16)
        v_s[R:KEYS, :] = jnp.zeros((KEYS - R, QUAD), BF16)

    hb = hb_ref[...]
    q4 = (nn(hb, wq_ref[...]) + vq_ref[0:1, :]).astype(BF16)
    k4 = nn(hb, wk_ref[...]).astype(BF16)
    v4 = (nn(hb, wv_ref[...]) + vq_ref[1:2, :]).astype(BF16)
    q_ref[...] = q4
    k_ref[...] = k4
    v_ref[...] = v4
    k_s[0:R, :] = k4
    v_s[0:R, :] = v4
    key = lax.broadcasted_iota(jnp.int32, (1, KEYS), 1)
    bias = jnp.where(key < count, 0.0, NEG)
    twice = math.log(2.0) * math.sqrt(HEAD_DIM)
    bias = jnp.where((key >= SEG) & (key < SEG + MEM), twice, bias)
    first = lax.broadcasted_iota(jnp.int32, (1, 128), 1) < HEAD_DIM
    one = jnp.ones((KEYS, 128), BF16)
    for pair in range(2):
        lanes = slice(128 * pair, 128 * pair + 128)
        q2 = q4[:, lanes]
        k2 = k_s[:, lanes]
        vx = jnp.concatenate([v_s[:, lanes], one], axis=1)
        outs = []
        for half in range(2):
            mine = first if half == 0 else jnp.logical_not(first)
            qh = jnp.where(mine, q2, jnp.zeros_like(q2))
            s = nt(qh, k2) + bias
            top = jnp.max(s, axis=-1, keepdims=True)
            e = jnp.exp2((s - top) * EXP_SCALE).astype(BF16)
            e_ref[2 * pair + half] = e
            outs.append(nn(e, vx))
        num = jnp.where(first, outs[0][:, :128], outs[1][:, :128])
        den = jnp.where(first, outs[0][:, 128:], outs[1][:, 128:])
        inv = 1.0 / den
        linv_ref[:, lanes] = inv
        o_ref[:, lanes] = (num * inv).astype(BF16)
    part = nn(o_ref[...], wo_ref[...])

    @pl.when(step == 0)
    def _():
        acc_s[...] = part

    @pl.when(step > 0)
    def _():
        acc_s[...] = acc_s[...] + part

    @pl.when(step == NQ - 1)
    def _():
        r = h_s[...] + (acc_s[...] + vec_ref[2:3, :])
        c = r - row_mean(r)
        rstd = lax.rsqrt(row_mean(c * c) + EPS)
        xhat_ref[...] = c * rstd
        rstd_ref[...] = jnp.broadcast_to(rstd, (R, 128))


def const(shape):
    return pl.BlockSpec(shape, lambda j, *_: (0,) * len(shape))


def cols(rows, width):
    return pl.BlockSpec((rows, width), lambda j, *_: (0, j))


def rows(height, width):
    return pl.BlockSpec((height, width), lambda j, *_: (j, 0))


def slot_const(slot):
    return pl.BlockSpec((R, D), lambda j, *_: (slot, 0))


def slot_cols(slot, width):
    return pl.BlockSpec((R, width), lambda j, *_: (slot, j))


def any_spec():
    return pl.BlockSpec(memory_space=pl.ANY)


def sds(shape, dtype):
    return jax.ShapeDtypeStruct(shape, dtype)


def kept(n, kernel):
    def body(*refs):
        return kernel(*refs[:1], *refs[1 + n :])

    return body


def cost(flops, moved):
    return pl.CostEstimate(flops=flops, bytes_accessed=moved, transcendentals=0)


def params():
    return pltpu.CompilerParams(
        dimension_semantics=("arbitrary",), vmem_limit_bytes=VMEM_LIMIT
    )


def attn_fwd(slot, slots, prev, count, tok, mem, wqk, wvo, vecs):
    n = len(prev)
    return pl.pallas_call(
        kept(n, attn_fwd_kernel),
        grid_spec=pltpu.PrefetchScalarGridSpec(
            num_scalar_prefetch=1,
            grid=(NQ,),
            in_specs=[any_spec()] * n + [
                pl.BlockSpec((SEG, D), lambda j, *_: (slot, 0)), const((MPAD, D)),
                cols(D, QUAD), pl.BlockSpec((D, QUAD), lambda j, *_: (0, NQ + j)),
                cols(D, QUAD), pl.BlockSpec((QUAD, D), lambda j, *_: (j, 1)),
                cols(8, QUAD), const((8, D)),
            ],
            out_specs=[
                slot_const(slot), cols(R, QUAD), cols(R, QUAD), cols(R, QUAD),
                slot_cols(slot, QUAD),
                cols(R, QUAD),
                pl.BlockSpec((4, R, KEYS), lambda j, *_: (j, 0, 0)),
                const((R, D)), const((R, 128)),
            ],
            scratch_shapes=[
                pltpu.VMEM((R, D), F32), pltpu.VMEM((KEYS, QUAD), BF16),
                pltpu.VMEM((KEYS, QUAD), BF16), pltpu.VMEM((R, D), F32),
            ],
        ),
        out_shape=[
            sds((slots * R, D), BF16), sds((R, D), BF16), sds((R, D), BF16), sds((R, D), BF16),
            sds((slots * R, D), BF16), sds((R, D), F32), sds((HEADS, R, KEYS), BF16),
            sds((R, D), F32), sds((R, 128), F32),
        ],
        input_output_aliases={1: 0, 2: 4} if n else {},
        compiler_params=params(),
        cost_estimate=cost(2 * R * (4 * D * D + 2 * KEYS * D * 4), 20_000_000),
        name="attn_fwd",
    )(count, *prev, tok, mem, wqk, wqk, wvo, wvo, vecs, vecs)


def norm_pull(grad, gain, xhat, rstd):
    gx = grad * gain
    return rstd * (gx - row_mean(gx) - xhat * row_mean(gx * xhat))


def attn_bwd_kernel(
    count_ref, dr1_ref, dr1b_ref, wq_ref, wk_ref, wv_ref, wo_ref, q_ref, k_ref, v_ref, o_ref,
    linv_ref, e_ref,
    dq_ref, dk_ref, dv_ref, dqb_ref, dvb_ref, gtok_ref, gmem_ref,
    k_s, v_s, acc_s,
):
    step = pl.program_id(0)

    @pl.when(step == 0)
    def _():
        k_s[R:KEYS, :] = jnp.zeros((KEYS - R, QUAD), BF16)
        v_s[R:KEYS, :] = jnp.zeros((KEYS - R, QUAD), BF16)
        acc_s[...] = dr1_ref[...]

    k_s[0:R, :] = k_ref[...]
    v_s[0:R, :] = v_ref[...]
    grad_o = nt(dr1b_ref[...], wo_ref[...]).astype(BF16).astype(F32) * linv_ref[...]
    grad_ob = grad_o.astype(BF16)
    term = (-(grad_o * o_ref[...].astype(F32))).astype(BF16)
    first = lax.broadcasted_iota(jnp.int32, (1, 128), 1) < HEAD_DIM
    one = jnp.ones((KEYS, 128), BF16)
    scaling = 1.0 / math.sqrt(HEAD_DIM)
    for pair in range(2):
        lanes = slice(128 * pair, 128 * pair + 128)
        q2 = q_ref[:, lanes]
        k2 = k_s[:, lanes]
        do2 = grad_ob[:, lanes]
        tm2 = term[:, lanes]
        vx = jnp.concatenate([v_s[:, lanes], one], axis=1)
        dqs, dks, dvs = [], [], []
        for half in range(2):
            mine = first if half == 0 else jnp.logical_not(first)
            zero = jnp.zeros_like(do2)
            lhs = jnp.concatenate([jnp.where(mine, do2, zero), jnp.where(mine, tm2, zero)], axis=1)
            e = e_ref[2 * pair + half]
            ds = (nt(lhs, vx) * e.astype(F32)).astype(BF16)
            dqs.append(nn(ds, k2))
            dks.append(tn(ds, q2))
            dvs.append(tn(e, do2))
        dq_ref[:, lanes] = (jnp.where(first, dqs[0], dqs[1]) * scaling).astype(BF16)
        dk_ref[:, lanes] = (jnp.where(first, dks[0], dks[1])[0:R, :] * scaling).astype(BF16)
        dv_ref[:, lanes] = jnp.where(first, dvs[0], dvs[1])[0:R, :].astype(BF16)
    dq = dq_ref[...]
    dv = dv_ref[...]
    dqb_ref[...] = col_sum(dq.astype(F32))
    dvb_ref[...] = col_sum(dv.astype(F32))
    part = nt(dq, wq_ref[...]) + nt(dk_ref[...], wk_ref[...]) + nt(dv, wv_ref[...])
    acc_s[...] = acc_s[...] + part

    @pl.when(step == NQ - 1)
    def _():
        live = row_ids(SEG, D) < count_ref[0]
        gtok_ref[...] = jnp.where(live, acc_s[0:SEG, :], 0.0)
        gmem_ref[...] = jnp.where(row_ids(MPAD, D) < MEM, acc_s[SEG:R, :], 0.0)


def attn_bwd(slot, slots, prev, count, dr1, dr1b, wqk, wvo, q, k, v, o, linv, e):
    n = len(prev)
    return pl.pallas_call(
        kept(n, attn_bwd_kernel),
        grid_spec=pltpu.PrefetchScalarGridSpec(
            num_scalar_prefetch=1,
            grid=(NQ,),
            in_specs=[any_spec()] * n + [
                const((R, D)), slot_const(slot),
                cols(D, QUAD), pl.BlockSpec((D, QUAD), lambda j, *_: (0, NQ + j)),
                cols(D, QUAD), pl.BlockSpec((QUAD, D), lambda j, *_: (j, 1)),
                cols(R, QUAD), cols(R, QUAD), cols(R, QUAD), slot_cols(slot, QUAD),
                cols(R, QUAD),
                pl.BlockSpec((4, R, KEYS), lambda j, *_: (j, 0, 0)),
            ],
            out_specs=[
                slot_cols(slot, QUAD), slot_cols(slot, QUAD), slot_cols(slot, QUAD),
                cols(1, QUAD), cols(1, QUAD),
                pl.BlockSpec((SEG, D), lambda j, *_: (slot, 0)), const((MPAD, D)),
            ],
            scratch_shapes=[
                pltpu.VMEM((KEYS, QUAD), BF16), pltpu.VMEM((KEYS, QUAD), BF16),
                pltpu.VMEM((R, D), F32),
            ],
        ),
        out_shape=[
            sds((slots * R, D), BF16), sds((slots * R, D), BF16), sds((slots * R, D), BF16),
            sds((1, D), F32), sds((1, D), F32), sds((slots * SEG, D), F32), sds((MPAD, D), F32),
        ],
        input_output_aliases={1: 0, 2: 1, 3: 2, 4: 5} if n else {},
        compiler_params=params(),
        cost_estimate=cost(2 * R * (4 * D * D + 5 * KEYS * D * 4), 20_000_000),
        name="attn_bwd",
    )(count, *prev, dr1, dr1b, wqk, wqk, wvo, wvo, q, k, v, o, linv, e)


MID_BF = 1536


def mid_kernel(
    pieces, info_ref, xhat0_ref, rstd0_ref, init_ref, vec_ref, bi_ref, *refs
):
    wi_hbm, refs = refs[:pieces], refs[pieces:]
    wu_hbm, refs = refs[:pieces], refs[pieces:]
    mid_body(
        info_ref, xhat0_ref, rstd0_ref, init_ref, vec_ref, bi_ref, wi_hbm, wu_hbm, *refs
    )


def mid_body(
    info_ref, xhat0_ref, rstd0_ref, init_ref, vec_ref, bi_ref, wi_hbm, wu_hbm,
    wqk_hbm, wvo_hbm, tok_hbm, cot_hbm, hb_in, o_in,
    mixed_hbm, hb_hbm, o_hbm, mine_hbm, theirs_hbm, g_hbm, df2_hbm, da_hbm,
    dq_hbm, dk_hbm, dv_hbm, gtok_hbm, dr1_hbm, gmem_ref, dvec_ref, dbi_ref,
    wqk_s, wvo_s, wi_s, wu_s, gp_s, g_s, xhat_s, xhat2_s, rstd_s, rstd2_s, h1b_s,
    hb_s, q_s, k_s, v_s, o_s, linv_s, e_s, h_s, acc_s, df2_s, da_s, tok_s, cot_s, mixed_s, mem_s,
    sems,
):
    used = [0]

    def copy(src, dst):
        used[0] += 1
        return pltpu.make_async_copy(src, dst, sems.at[used[0] - 1])

    half = FF // 2
    core = info_ref[3]

    if len(wi_hbm) == 1:
        wi_spots = [(wi_hbm[0], wi_s)]
        wu_spots = [(wu_hbm[0], wu_s)]
    else:
        wi_spots = [
            (a, wi_s.at[:, info_ref[4] ^ (i % 2), core ^ (i // 2)])
            for i, a in enumerate(wi_hbm)
        ]
        wu_spots = [
            (a, wu_s.at[:, core ^ (i // 2), info_ref[5] ^ (i % 2)])
            for i, a in enumerate(wu_hbm)
        ]

    def rest(ref):
        return (slice(None),) * (len(ref.shape) - 1)

    in_wi = [
        [
            copy(a.at[(*rest(a), pl.ds(half * i, half))], b.at[(*rest(b), pl.ds(half * i, half))])
            for a, b in wi_spots
        ]
        for i in range(2)
    ]
    in_wu = [
        [copy(a.at[4 * i : 4 * i + 4], b.at[4 * i : 4 * i + 4]) for a, b in wu_spots]
        for i in range(2)
    ]
    in_tok = copy(tok_hbm.at[SEG : 2 * SEG], tok_s)
    in_wqk = copy(wqk_hbm, wqk_s)
    in_wvo = copy(wvo_hbm.at[:, 0 : 2 * D], wvo_s)
    in_cot1 = copy(cot_hbm.at[SEG : 2 * SEG], cot_s)
    for c in (*in_wi[0], *in_wu[0], *in_wi[1], *in_wu[1], in_tok, in_wqk, in_wvo, in_cot1):
        c.start()
    xhat_s[0] = xhat0_ref[...]
    rstd_s[0] = rstd0_ref[...]
    k_s[R:KEYS, :] = jnp.zeros((KEYS - R, D), BF16)
    v_s[R:KEYS, :] = jnp.zeros((KEYS - R, D), BF16)
    first = lax.broadcasted_iota(jnp.int32, (1, 128), 1) < HEAD_DIM
    one = jnp.ones((KEYS, 128), BF16)

    def row(i):
        return vec_ref[i : i + 1, :]

    def lanes(start, size):
        return pl.ds(pl.multiple_of(start, size), size)

    def wi_at(at):
        return wi_s[:, :, :, :, at].reshape(D, MID_BF)

    def wu_at(j):
        size = MID_BF * 8 // FF
        return wu_s[pl.ds(j * size, size)].reshape(MID_BF, D)

    def feed_forward(seg):
        h1 = xhat_s[seg] * row(3) + row(4)
        h1b_s[seg] = h1.astype(BF16)
        acc_s[...] = h1 + row(5)

        def chunk(j, carry):
            at = lanes(j * MID_BF, MID_BF)
            f1 = nn(h1b_s[seg], wi_at(at)) + bi_ref[:, at]
            cdf = 0.5 * (1.0 + lax.erf(f1 * math.sqrt(0.5)))
            pdf = jnp.exp(-0.5 * f1 * f1) * (1.0 / math.sqrt(2.0 * math.pi))
            g = (f1 * cdf).astype(BF16)
            g_s[:, at] = g
            gp_s[seg, :, at] = (cdf + f1 * pdf).astype(BF16)
            acc_s[...] = acc_s[...] + nn(g, wu_at(j))
            return carry

        n = half // MID_BF
        if seg == 0:
            for c in in_wi[0] + in_wu[0]:
                c.wait()
        lax.fori_loop(0, n, chunk, 0)
        if seg == 0:
            for c in in_wi[1] + in_wu[1]:
                c.wait()
        lax.fori_loop(n, 2 * n, chunk, 0)
        r = acc_s[...]
        c = r - row_mean(r)
        rstd = lax.rsqrt(row_mean(c * c) + EPS)
        xhat = c * rstd
        xhat2_s[seg] = xhat
        rstd2_s[seg] = jnp.broadcast_to(rstd, (R, 128))
        y = xhat * row(6) + row(7)
        live = row_ids(SEG, D) < info_ref[seg]
        mixed_s[...] = jnp.where(live, y[0:SEG, :], 0.0).astype(BF16)
        if seg == 0:
            write = jnp.where(row_ids(MPAD, D) < MEM, y[SEG:R, :], 0.0)
            mem_s[...] = jnp.where(info_ref[2] > 0, init_ref[...], write)

    def feed_forward_back(seg, grad_write):
        live = row_ids(SEG, D) < info_ref[seg]
        acc_s[0:SEG, :] = jnp.where(live, cot_s[...].astype(F32), 0.0)
        acc_s[SEG:R, :] = grad_write
        dy = acc_s[...]
        xhat2 = xhat2_s[seg]
        sums = [col_sum(dy * xhat2), col_sum(dy)]
        dr2 = norm_pull(dy, row(6), xhat2, rstd2_s[seg, :, 0:1])
        df2 = dr2.astype(BF16)
        df2_s[...] = df2
        sums.insert(0, col_sum(df2.astype(F32)))
        acc_s[...] = dr2

        def chunk(j, carry):
            at = lanes(j * MID_BF, MID_BF)
            df1 = (nt(df2_s[...], wu_at(j)) * gp_s[seg, :, at].astype(F32)).astype(BF16)
            gp_s[seg, :, at] = df1
            total = col_sum(df1.astype(F32))
            dbi_ref[:, at] = total if seg == 1 else dbi_ref[:, at] + total
            acc_s[...] = acc_s[...] + nt(df1, wi_at(at))
            return carry

        lax.fori_loop(0, FF // MID_BF, chunk, 0)
        dh1 = acc_s[...]
        xhat = xhat_s[seg]
        sums = [col_sum(dh1 * xhat), col_sum(dh1)] + sums
        dr1 = norm_pull(dh1, row(3), xhat, rstd_s[seg, :, 0:1])
        acc_s[...] = dr1
        da = dr1.astype(BF16)
        da_s[...] = da
        sums = [col_sum(da.astype(F32))] + sums
        for i, total in enumerate(sums):
            at = slice(2 + i, 3 + i)
            dvec_ref[at, :] = total if seg == 1 else dvec_ref[at, :] + total

    feed_forward(0)
    outs = {}

    def send(name, src, dst):
        outs[name] = copy(src, dst)
        outs[name].start()

    def done(*names):
        for name in names:
            outs.pop(name).wait()

    send("g0", g_s, g_hbm.at[0:R])
    send("mixed0", mixed_s, mixed_hbm.at[0:SEG])

    in_tok.wait()
    live = row_ids(SEG, D) < info_ref[1]
    h_s[0:SEG, :] = jnp.where(live, tok_s[...].astype(F32), 0.0)
    h_s[SEG:R, :] = mem_s[...]
    hb_s[...] = h_s[...].astype(BF16)
    send("hb", hb_s, hb_hbm.at[R : 2 * R])
    in_wqk.wait()
    in_wvo.wait()
    key = lax.broadcasted_iota(jnp.int32, (1, KEYS), 1)
    bias = jnp.where(key < info_ref[1], 0.0, NEG)
    twice = math.log(2.0) * math.sqrt(HEAD_DIM)
    bias = jnp.where((key >= SEG) & (key < SEG + MEM), twice, bias)

    qk = nn(hb_s[...], wqk_s[...])
    q_s[...] = (qk[:, :D] + row(0)).astype(BF16)
    k_s[0:R, :] = qk[:, D:].astype(BF16)
    v_s[0:R, :] = (nn(hb_s[...], wvo_s[:, :D]) + row(1)).astype(BF16)

    def quad_forward(j, carry):
        for pair in range(2):
            here = lanes(j * QUAD + 128 * pair, 128)
            q2 = q_s[:, here]
            k2 = k_s[:, here]
            vx = jnp.concatenate([v_s[:, here], one], axis=1)
            parts = []
            for side in range(2):
                mine = first if side == 0 else jnp.logical_not(first)
                s = nt(jnp.where(mine, q2, jnp.zeros_like(q2)), k2) + bias
                top = jnp.max(s, axis=-1, keepdims=True)
                e = jnp.exp2((s - top) * EXP_SCALE).astype(BF16)
                e_s[4 * j + 2 * pair + side] = e
                parts.append(nn(e, vx))
            num = jnp.where(first, parts[0][:, :128], parts[1][:, :128])
            den = jnp.where(first, parts[0][:, 128:], parts[1][:, 128:])
            inv = 1.0 / den
            linv_s[:, here] = inv
            o_s[:, here] = (num * inv).astype(BF16)
        return carry

    lax.fori_loop(0, NQ, quad_forward, 0)
    send("o", o_s, o_hbm.at[R : 2 * R])
    r = h_s[...] + (nn(o_s[...], wvo_s[:, D:]) + row(2))
    c = r - row_mean(r)
    rstd = lax.rsqrt(row_mean(c * c) + EPS)
    xhat_s[1] = c * rstd
    rstd_s[1] = jnp.broadcast_to(rstd, (R, 128))

    done("g0", "mixed0")
    feed_forward(1)
    send("g1", g_s, g_hbm.at[R : 2 * R])
    send("mixed1", mixed_s, mixed_hbm.at[SEG : 2 * SEG])

    in_cot1.wait()
    feed_forward_back(1, jnp.zeros((MPAD, D), F32))
    in_cot0 = copy(cot_hbm.at[0:SEG], cot_s)
    in_cot0.start()
    send("df2", df2_s, df2_hbm.at[R : 2 * R])
    send("da", da_s, da_hbm.at[R : 2 * R])

    scaling = 1.0 / math.sqrt(HEAD_DIM)
    done("hb", "o", "g1")
    grad_o = nt(da_s[...], wvo_s[:, D:]).astype(BF16).astype(F32) * linv_s[...]
    g_s[:, 0:D] = grad_o.astype(BF16)
    g_s[:, D : 2 * D] = (-(grad_o * o_s[...].astype(F32))).astype(BF16)

    def quad_back(j, carry):
        for pair in range(2):
            here = lanes(j * QUAD + 128 * pair, 128)
            q2 = q_s[:, here]
            k2 = k_s[:, here]
            do2 = g_s[:, here]
            tm2 = g_s[:, lanes(D + j * QUAD + 128 * pair, 128)]
            vx = jnp.concatenate([v_s[:, here], one], axis=1)
            dqs, dks, dvs = [], [], []
            for side in range(2):
                mine = first if side == 0 else jnp.logical_not(first)
                zero = jnp.zeros_like(do2)
                lhs = jnp.concatenate(
                    [jnp.where(mine, do2, zero), jnp.where(mine, tm2, zero)], axis=1
                )
                e = e_s[4 * j + 2 * pair + side]
                ds = (nt(lhs, vx) * e.astype(F32)).astype(BF16)
                dqs.append(nn(ds, k2))
                dks.append(tn(ds, q2))
                dvs.append(tn(e, do2))
            q_s[:, here] = (jnp.where(first, dqs[0], dqs[1]) * scaling).astype(BF16)
            k_s[0:R, here] = (jnp.where(first, dks[0], dks[1])[0:R, :] * scaling).astype(BF16)
            v_s[0:R, here] = jnp.where(first, dvs[0], dvs[1])[0:R, :].astype(BF16)
        return carry

    lax.fori_loop(0, NQ, quad_back, 0)
    dvec_ref[0:1, :] = col_sum(q_s[...].astype(F32))
    dvec_ref[1:2, :] = col_sum(v_s[0:R, :].astype(F32))
    part = nt(q_s[...], wqk_s[:, :D]) + nt(k_s[0:R, :], wqk_s[:, D:])
    acc_s[...] = acc_s[...] + (part + nt(v_s[0:R, :], wvo_s[:, :D]))
    send("dq", q_s, dq_hbm.at[R : 2 * R])
    send("dk", k_s.at[0:R], dk_hbm.at[R : 2 * R])
    send("dv", v_s.at[0:R], dv_hbm.at[R : 2 * R])
    h_s[0:SEG, :] = jnp.where(live, acc_s[0:SEG, :], 0.0)
    send("gtok", h_s.at[0:SEG], gtok_hbm.at[SEG : 2 * SEG])
    grad_mem = jnp.where(row_ids(MPAD, D) < MEM, acc_s[SEG:R, :], 0.0)
    gmem_ref[...] = grad_mem
    in_cot0.wait()
    done("df2", "da")
    feed_forward_back(0, jnp.where(info_ref[2] > 0, 0.0, grad_mem))
    send("df2", df2_s, df2_hbm.at[0:R])
    send("da", da_s, da_hbm.at[0:R])
    send("dr1", acc_s, dr1_hbm)

    def weight_grad(j, carry):
        at = lanes(j * D, D)
        left = h1b_s[...].reshape(2 * R, D)
        total = tn(left, gp_s[:, :, at].reshape(2 * R, D))
        wi_s[:, :, :, :, at] = total.astype(BF16).reshape(wi_s.shape[:4] + (D,))
        return carry

    lax.fori_loop(0, FF // D, weight_grad, 0)
    send("mine", wi_s.at[:, :, :, :, lanes(core * half, half)], mine_hbm)
    send("theirs", wi_s.at[:, :, :, :, lanes((1 - core) * half, half)], theirs_hbm)
    done(*list(outs))


def mid(info, xhat0, rstd0, init, vecs, bi, wi, wu, wqk, wvo, tok, cot, hb, o):
    whole = pl.BlockSpec(memory_space=pltpu.VMEM)
    smem = pl.BlockSpec(memory_space=pltpu.SMEM)
    two, n = 2 * R, len(wi)
    wide = (4, 2, 2, D // 16)
    return pl.pallas_call(
        functools.partial(mid_kernel, n),
        in_specs=[smem] + [whole] * 5 + [any_spec()] * (6 + 2 * n),
        out_specs=[any_spec()] * 13 + [whole] * 3,
        out_shape=[
            sds((2 * SEG, D), BF16), sds((two, D), BF16), sds((two, D), BF16),
            sds(wide + (FF // 2,), BF16), sds(wide + (FF // 2,), BF16),
            sds((two, FF), BF16), sds((two, D), BF16), sds((two, D), BF16),
            sds((two, D), BF16), sds((two, D), BF16), sds((two, D), BF16),
            sds((2 * SEG, D), F32), sds((R, D), F32),
            sds((MPAD, D), F32), sds((8, D), F32), sds((1, FF), F32),
        ],
        scratch_shapes=[
            pltpu.VMEM((D, 2 * D), BF16), pltpu.VMEM((D, 2 * D), BF16),
            pltpu.VMEM(wide + (FF,), BF16), pltpu.VMEM((8, 2, 2, FF // 32, D), BF16),
            pltpu.VMEM((2, R, FF), BF16), pltpu.VMEM((R, FF), BF16),
            pltpu.VMEM((2, R, D), F32), pltpu.VMEM((2, R, D), F32),
            pltpu.VMEM((2, R, 128), F32), pltpu.VMEM((2, R, 128), F32),
            pltpu.VMEM((2, R, D), BF16),
            pltpu.VMEM((R, D), BF16), pltpu.VMEM((R, D), BF16), pltpu.VMEM((KEYS, D), BF16),
            pltpu.VMEM((KEYS, D), BF16), pltpu.VMEM((R, D), BF16), pltpu.VMEM((R, D), F32),
            pltpu.VMEM((HEADS, R, KEYS), BF16),
            pltpu.VMEM((R, D), F32), pltpu.VMEM((R, D), F32),
            pltpu.VMEM((R, D), BF16), pltpu.VMEM((R, D), BF16),
            pltpu.VMEM((SEG, D), BF16), pltpu.VMEM((SEG, D), BF16), pltpu.VMEM((SEG, D), BF16),
            pltpu.VMEM((MPAD, D), F32),
            pltpu.SemaphoreType.DMA((48,)),
        ],
        input_output_aliases={10 + 2 * n: 1, 11 + 2 * n: 2},
        compiler_params=pltpu.CompilerParams(vmem_limit_bytes=MID_LIMIT),
        cost_estimate=cost(2 * R * 48 * D * D + 14 * R * KEYS * D * 4, 60_000_000),
        name="mid",
    )(info, xhat0, rstd0, init, vecs, bi, *wi, *wu, wqk, wvo, tok, cot, hb, o)


def wgrad_outer_kernel(core_ref, g_ref, d_ref, mine_ref, theirs_ref):
    full = tn(g_ref[...], d_ref[...]).astype(BF16)
    low = core_ref[0] == 0
    left, right = full[:, : D // 2], full[:, D // 2 :]
    mine_ref[...] = jnp.where(low, left, right)
    theirs_ref[...] = jnp.where(low, right, left)


def wgrad_outer(core, g, d):
    depth, n = g.shape[0], FF // D
    return pl.pallas_call(
        wgrad_outer_kernel,
        grid_spec=pltpu.PrefetchScalarGridSpec(
            num_scalar_prefetch=1,
            grid=(n,),
            in_specs=[cols(depth, D), const((depth, D))],
            out_specs=[rows(D, D // 2), rows(D, D // 2)],
        ),
        out_shape=[sds((FF, D // 2), BF16)] * 2,
        compiler_params=params(),
        cost_estimate=cost(2 * depth * D * FF * 2, 15_000_000),
        name="wgrad_outer",
    )(core, g, d)


def wgrad_attn_kernel(
    core_ref, hb_ref, o_ref, dq_ref, dk_ref, dv_ref, da_ref, qv_ref, vq_ref, ko_ref, ok_ref
):
    low = core_ref[0] == 0

    def put(mine_ref, theirs_ref, left, right):
        mine_ref[...] = jnp.where(low, left, right)
        theirs_ref[...] = jnp.where(low, right, left)

    dq, dk = tn(hb_ref[...], dq_ref[...]), tn(hb_ref[...], dk_ref[...])
    dv, do = tn(hb_ref[...], dv_ref[...]), tn(o_ref[...], da_ref[...])
    put(qv_ref, vq_ref, dq.astype(BF16), dv.astype(BF16))
    put(ko_ref, ok_ref, dk.astype(BF16), do.astype(BF16))


def wgrad_attn(core, hb, o, dq, dk, dv, da):
    depth, n = hb.shape[0], D // QUAD
    return pl.pallas_call(
        wgrad_attn_kernel,
        grid_spec=pltpu.PrefetchScalarGridSpec(
            num_scalar_prefetch=1,
            grid=(n,),
            in_specs=[const((depth, D))] * 2 + [cols(depth, QUAD)] * 4,
            out_specs=[cols(D, QUAD)] * 4,
        ),
        out_shape=[sds((D, D), BF16)] * 4,
        compiler_params=params(),
        cost_estimate=cost(2 * depth * D * D * 4 * 2, 15_000_000),
        name="wgrad_attn",
    )(core, hb, o, dq, dk, dv, da)


def strides(size):
    return [1 << i for i in reversed(range(size.bit_length() - 1))]


def after(value, *others):
    return lax.optimization_barrier((value, others))[0]


class Cube:
    def __init__(self, wide, narrow):
        self.size = {"wide": wide, "narrow": narrow}
        self.dims = [("wide", s) for s in strides(wide)] + [("narrow", s) for s in strides(narrow)]
        self.core, self.y, self.x = ("wide", 1), ("wide", 2), ("narrow", 1)
        self.rest = [d for d in self.dims if d not in (self.core, self.y, self.x)]

    def bit(self, dim):
        return (lax.axis_index(dim[0]) // dim[1]) % 2

    def swap(self, value, dim):
        axis, stride = dim
        return lax.ppermute(value, axis, [(i, i ^ stride) for i in range(self.size[axis])])

    def open(self, value):
        return value.reshape((1,) * len(self.dims) + value.shape)

    def join(self, value, got, dim):
        low = self.bit(dim) == 0
        return jnp.concatenate(
            [jnp.where(low, value, got), jnp.where(low, got, value)], axis=self.dims.index(dim)
        )

    def grow(self, value, *dims):
        for dim in dims:
            value = self.join(value, self.swap(value, dim), dim)
        return value

    def add(self, mine, got):
        return (mine.astype(F32) + got.astype(F32)).astype(mine.dtype)

    def split(self, value, dim):
        axis, bit = self.dims.index(dim), self.bit(dim)
        return (
            lax.dynamic_index_in_dim(value, bit, axis),
            lax.dynamic_index_in_dim(value, 1 - bit, axis),
        )

    def shrink(self, value, *dims):
        for dim in dims:
            mine, theirs = self.split(value, dim)
            value = self.add(mine, self.swap(theirs, dim))
        return value

    def phase(self, *items):
        parts = [self.split(value, dim) for value, dim in items]
        sends = lax.optimization_barrier([p[1] for p in parts])
        gots = [self.swap(send, dim) for send, (_, dim) in zip(sends, items)]
        gots = lax.optimization_barrier(gots)
        return [self.add(p[0], got) for p, got in zip(parts, gots)]

    def spread(self, value):
        return value.reshape((2,) * len(self.dims) + (-1, value.shape[-1]))

    def halves(self, value):
        mine, theirs = self.split(value, self.core)
        got = self.swap(theirs, self.core)
        low = self.bit(self.core) == 0
        width = value.shape[-1]
        return (
            jnp.where(low, mine, got).reshape(-1, width),
            jnp.where(low, got, mine).reshape(-1, width),
        )


def lanes_of(vec, own, groups):
    n = vec.shape[-1]
    height = -(-n // 128)
    vec = jnp.pad(vec.reshape(groups, n), ((0, 0), (0, height * 128 - n)))
    vec = vec.reshape(groups, height, 128)
    return jnp.pad(vec, ((0, 0), (0, own - height), (0, 0))).reshape(groups * own, 128)


def lanes_back(block, own, groups, n):
    height = -(-n // 128)
    return block.reshape(groups, own, 128)[:, :height].reshape(groups, height * 128)[:, :n]


def per_device(
    sizes, tokens, init_memory, w_query, w_key, w_value, w_output, w_inner, w_outer, vectors,
    chain_start, true_count, cotangent,
):
    cube = Cube(*sizes)
    core = cube.bit(cube.core).reshape(1)
    slots = chain_start.shape[0]
    parts = D * D // w_query.shape[0]
    own = D // parts
    n_vec = vectors.shape[0]
    square = [w.reshape(own, D) for w in (w_query, w_key, w_value, w_output)]
    wqk = cube.open(jnp.concatenate(square[:2], axis=1))
    wvo = cube.open(jnp.concatenate(square[2:] + [lanes_of(vectors, own, 1)], axis=1))
    wi = cube.open(w_inner.reshape(own, FF))
    wu = cube.open(w_outer.reshape(FF // parts, D))
    wqk, wvo = cube.grow(wqk, *cube.rest), cube.grow(wvo, *cube.rest)
    wi, wu = cube.grow(after(wi, wqk), *cube.rest), cube.grow(after(wu, wvo), *cube.rest)
    wqk, wvo = cube.grow(wqk, cube.y, cube.x), cube.grow(wvo, cube.x, cube.y)
    wi, wu = cube.grow(after(wi, wqk), cube.x), cube.grow(after(wu, wvo), cube.y)
    wqk, wvo = cube.grow(wqk, cube.core), cube.grow(wvo, cube.core)
    wqk, wvo = after(wqk, wi), after(wvo, wu)
    wqk, wvo = wqk.reshape(D, -1), wvo.reshape(D, -1)
    wi_got, wu_got = cube.swap(wi, cube.y), cube.swap(wu, cube.x)
    wi_core, wu_core = cube.swap(wi, cube.core), cube.swap(wu, cube.core)
    vec_all = lanes_back(wvo[:, 2 * D :], own, parts, n_vec).reshape(-1).astype(F32)
    vecs = vec_all[: 8 * D].reshape(8, D)
    bi = vec_all[8 * D :].reshape(1, FF)

    init = jnp.pad(init_memory.astype(F32), ((0, 0), (0, MPAD - MEM), (0, 0)))
    count = true_count[0:1]
    hb, q, k, v, o, linv, e, xhat, rstd = attn_fwd(
        0, slots, [], count, tokens, init[0], wqk, wvo, vecs
    )
    wi_got, wu_got, wi_core, wu_core = after((wi_got, wu_got, wi_core, wu_core), xhat)
    wi = [wi, wi_got, wi_core, cube.swap(wi_got, cube.core)]
    wu = [wu, wu_got, wu_core, cube.swap(wu_got, cube.core)]
    if D // parts * 2 % 16 == 0 and sizes == (16, 2):
        wi = [w.reshape(4, D // 16, FF) for w in wi]
        wu = [w.reshape(8, FF // 32, D) for w in wu]
    else:
        wi = [cube.join(wi[i], wi[i + 1], cube.y) for i in (0, 2)]
        wu = [cube.join(wu[i], wu[i + 1], cube.x) for i in (0, 2)]
        wi = [cube.join(*wi, cube.core).reshape(4, 2, 2, D // 16, FF)]
        wu = [cube.join(*wu, cube.core).reshape(8, 2, 2, FF // 32, D)]
    info = jnp.concatenate(
        [true_count, chain_start[1:2], core, cube.bit(cube.y)[None], cube.bit(cube.x)[None]]
    )
    (
        mixed, hb, o, mine, theirs, g, df2, da, dq, dk, dv, grad_tokens, dr1, gmem, dvec, dbi,
    ) = mid(info, xhat, rstd, init[1], vecs, bi, wi, wu, wqk, wvo, tokens, cotangent, hb, o)
    grad_init = [None, jnp.where(chain_start[1] > 0, gmem, 0.0)[:MEM]]
    mine, theirs = mine.reshape(D, FF // 2), theirs.reshape(D, FF // 2)
    inner_got = cube.swap(theirs, cube.core)
    outer = wgrad_outer(core, g, df2)
    inner = cube.spread(cube.add(mine, after(inner_got, outer)))
    outer = cube.spread(cube.add(outer[0], cube.swap(outer[1], cube.core)))
    inner, inner_send = cube.split(inner, cube.x)
    outer, outer_send = cube.split(outer, cube.y)
    dr1 = after(dr1, inner_send, outer_send)
    inner_got = cube.swap(inner_send, cube.x)
    outer_got = cube.swap(outer_send, cube.y)
    dq, dk, dv, dqb, dvb, grad_tokens, gmem = attn_bwd(
        0, slots, [dq, dk, dv, grad_tokens], count, dr1, da, wqk, wvo, q, k, v, o, linv, e
    )
    grad_init[0] = gmem[:MEM]
    vec_parts = [
        jnp.concatenate([dvec.reshape(1, -1), dbi], axis=1),
        jnp.concatenate([dqb, dvb, jnp.zeros((1, 6 * D + FF), F32)], axis=1),
    ]
    inner = cube.add(inner, after(inner_got, dq))
    outer = cube.add(outer, after(outer_got, dq))
    inner, inner_send = cube.split(inner, cube.y)
    outer, outer_send = cube.split(outer, cube.x)
    attn = wgrad_attn(core, after(hb, inner_send, outer_send), o, dq, dk, dv, da)
    inner_got = cube.swap(inner_send, cube.y)
    outer_got = cube.swap(outer_send, cube.x)
    inner = cube.add(inner, after(inner_got, attn))
    outer = cube.add(outer, after(outer_got, attn))
    first_got, second_got = cube.swap(attn[1], cube.core), cube.swap(attn[3], cube.core)
    first = cube.spread(cube.add(attn[0], first_got))
    second = cube.spread(cube.add(attn[2], second_got))
    vec = sum(vec_parts).reshape((2,) * len(cube.dims) + (1, n_vec))
    order = cube.rest[::-1]
    first, second, inner, outer, vec = cube.phase(
        (first, cube.x), (second, cube.y), (inner, order[0]), (outer, order[0]), (vec, cube.core)
    )
    first, second, vec = cube.phase((first, cube.y), (second, cube.x), (vec, cube.x))
    inner, outer = cube.shrink(inner, *order[1:]), cube.shrink(outer, *order[1:])
    first, second, vec = cube.phase((first, order[0]), (second, order[0]), (vec, cube.y))
    first, second = cube.shrink(first, *order[1:]), cube.shrink(second, *order[1:])
    vec = cube.shrink(vec, *order)
    g_query, g_value = cube.halves(first)
    g_key, g_output = cube.halves(second)
    inner = jnp.concatenate(cube.halves(inner), axis=1)
    outer = jnp.concatenate(cube.halves(outer), axis=1)
    return (
        mixed,
        grad_tokens,
        jnp.stack(grad_init),
        *(
            piece.astype(F32).reshape(-1)
            for piece in (g_query, g_key, g_value, g_output, inner, outer, vec)
        ),
    )


AXES = ("wide", "narrow")


def solution(mesh):
    flat = P(AXES)
    sizes = (mesh.shape["wide"], mesh.shape["narrow"])
    return jax.shard_map(
        functools.partial(per_device, sizes),
        mesh=mesh,
        in_specs=(P(AXES, None), P(AXES, None, None)) + (flat,) * 9 + (P(AXES, None),),
        out_specs=(P(AXES, None), P(AXES, None), P(AXES, None, None)) + (flat,) * 7,
        check_vma=False,
    )
```
